128 devices in a mesh: pipe: 4 (over z), dp: 32 (over y, x, core).
Axes of the slice: x: 4, y: 4, z: 4, core: 2. Of those that a mesh axis runs over, the one named last changes fastest.
Arguments:
- acts: bfloat16 [4, 4096, 5120], P('pipe', 'dp'), may hold values from -6 to 6
- cotangent: bfloat16 [4096, 5120], P('dp'), may hold values from -0.59765625 to 0.59765625
- kv_grads: bfloat16 [4, 4096, 2048], P('pipe', 'dp'), may hold values from -6 to 6
- w_kv: bfloat16 [4, 5120, 2048], P('pipe'), may hold values from -0.0078125 to 0.0078125
- momentum: bfloat16 [4, 5120, 2048], P('pipe', 'dp'), may hold values from -0.119628906 to 0.119628906
Outputs:
- update: bfloat16 [4, 5120, 2048], P('pipe', 'dp')
- input_grads: bfloat16 [4, 4096, 5120], P('pipe', 'dp')
The draws below stay inside these ranges and needn't reach their ends.
All inputs are finite; a program needn't handle non-finite values.
Results may differ from the reference program's by a relative error of at most 0.022.
Values may be sent and summed in bfloat16 or wider, within the bound.
A program may use at most 128 MiB of HBM per device.

```python
import math
import jax
import jax.numpy as jnp
from jax import lax

D = 5120
HEAD = 128
TOK_DEV = 128
ITERS = 5
LAT = 1024
MATS = 16
SECTIONS = 4
TOKENS = 4096
N_DP = 32


def raised(entries, own_key, source, target, parts, factor):
    def block_of(dim):
        return (jnp.arange(entries.shape[dim]) // (entries.shape[dim] // parts)).reshape((-1,) + (1,) * (entries.ndim - 1 - dim))

    first = jax.random.permutation(own_key, parts)[block_of(target)]
    other_side = (block_of(target) + parts // 2) % parts
    return jnp.where((block_of(source) == first) | (block_of(source) == other_side), factor * entries, entries)


def steps_of(key, dims, shards, least, top_value):
    factor_of, own = 1.0, jax.random.fold_in(key, 6)
    for axis_at, parts in shards:
        steps = jnp.exp(jax.random.uniform(jax.random.fold_in(own, axis_at), (parts,), jnp.float32, least / len(shards), top_value / len(shards)))
        factor_of = factor_of * jnp.repeat(steps, dims[axis_at] // parts).reshape([-1 if axis == axis_at else 1 for axis in range(len(dims))])
    return factor_of


def gaussian(rng, dims, width, reach, shards=(), held_as=jnp.bfloat16):
    factor_of = steps_of(rng, dims, shards, -0.22, 0.18) if shards else 1.0
    array = jax.random.normal(rng, dims, jnp.float32) * width * factor_of
    return jnp.minimum(jnp.maximum(array, -reach), reach).astype(held_as)


def bell_draw_with(own_key, dims, scale, limit, cuts, heavy, kind=jnp.bfloat16):
    array = scale * jax.random.normal(own_key, dims, jnp.float32)
    if cuts:
        array = array * steps_of(own_key, dims, cuts, -0.22, 0.18)
    return jnp.clip(raised(array, jax.random.fold_in(own_key, 3), *heavy), -limit, limit).astype(kind)


def setup_inputs(seed: int = 0) -> dict:
    arg_keys = jax.random.split(jax.random.key(seed), 6)
    return {
        "acts": bell_draw_with(arg_keys[0], (SECTIONS, TOKENS, D), 1.0, 6.0, ((0, 4), (1, 32)), (1, 2, 32, 2.75)),
        "cotangent": gaussian(arg_keys[1], (TOKENS, D), 0.1, 0.59765625, ((0, 32),)),
        "kv_grads": gaussian(arg_keys[2], (SECTIONS, TOKENS, 2 * LAT), 1.0, 6.0, ((0, 4), (1, 32))),
        "w_kv": gaussian(arg_keys[3], (SECTIONS, D, 2 * LAT), (100 * D) ** -0.5, 0.0078125, ((0, 4),)),
        "momentum": gaussian(arg_keys[4], (SECTIONS, D, 2 * LAT), 0.02, 0.119628906, ((0, 4), (1, 32))),
    }


momentum_rate = 0.95
quintic_a = 3.4445
quintic_b = -4.775
quintic_c = 2.0315
epsilon = 1e-07

def layer_back(incoming, kv_rows, weights):
    return (incoming.astype(jnp.float32) + jnp.dot(kv_rows, weights.T, preferred_element_type=jnp.float32)).astype(jnp.bfloat16)

def partial_sums(inputs, kv_rows):

    def shaped(values):
        return values.reshape(N_DP, TOK_DEV, values.shape[1])

    def accumulate(total, pieces):
        rows_in, rows_kv = pieces
        term = jnp.dot(rows_in.T, rows_kv, preferred_element_type=jnp.float32) * (1.0 / TOKENS)
        rounded = lax.optimization_barrier(term.astype(jnp.bfloat16))
        return (total + rounded.astype(jnp.float32), None)
    start = jnp.zeros((D, 2 * LAT), jnp.float32)
    total, unused = lax.scan(accumulate, start, (shaped(inputs), shaped(kv_rows)))
    return total

def orthogonalize(buffer):
    values = buffer.astype(jnp.float32)
    squares = lax.optimization_barrier(jnp.sum(values * values, axis=(1, 2), keepdims=True))
    current = values / (jnp.sqrt(squares) + epsilon)
    highest = lax.Precision.HIGHEST
    for step in range(ITERS):
        gram = jnp.einsum('mri,mrj->mij', current, current, precision=highest)
        mixer = quintic_b * gram + quintic_c * jnp.einsum('mij,mjk->mik', gram, gram, precision=highest)
        current = quintic_a * current + jnp.einsum('mri,mij->mrj', current, mixer, precision=highest)
    return current

def reference(acts, cotangent, kv_grads, w_kv, momentum):
    scale = 0.2 * math.sqrt(max(D, HEAD))
    incoming = cotangent
    updates = [None] * SECTIONS
    grads = [None] * SECTIONS
    for section in reversed(range(SECTIONS)):
        outgoing = layer_back(incoming, kv_grads[section], w_kv[section])
        grad = partial_sums(acts[section], kv_grads[section])
        buffer = (momentum_rate * momentum[section].astype(jnp.float32) + grad).astype(jnp.bfloat16)
        matrices = buffer.reshape(D, MATS, HEAD).transpose(1, 0, 2)
        result = orthogonalize(matrices)
        final = (scale * result).astype(jnp.bfloat16)
        updates[section] = final.transpose(1, 0, 2).reshape(D, MATS * HEAD)
        grads[section] = outgoing
        incoming = outgoing
    return (jnp.stack(updates), jnp.stack(grads))
```

```python
import functools
import math

import jax
import jax.numpy as jnp
from jax import lax
from jax.experimental import pallas as pl
from jax.experimental.pallas import tpu as pltpu
from jax.sharding import PartitionSpec as P

MESH = pl.DeviceIdType.MESH
F32 = jnp.float32
BF16 = jnp.bfloat16
HEAD = 128
ITERS = 5
TOK = 128
D = 5120
COLS = 2048
HALF = 1024
ROWS = 320
OWN = 160
CH = 256
NCH = D // CH
ORDER = (2, 1, 3, 0)
FAR = (2, 1, 3)

momentum_rate = 0.95
quintic_a = 3.4445
quintic_b = -4.775
quintic_c = 2.0315
epsilon = 1e-07


def mod4(v):
    return lax.rem(v, 4)


def mm(a, b):
    return jnp.dot(a, b, preferred_element_type=F32, precision=lax.Precision.HIGHEST)


def newton_schulz(gram, scale):
    rows = lax.broadcasted_iota(jnp.int32, (HEAD, HEAD), 0)
    cols = lax.broadcasted_iota(jnp.int32, (HEAD, HEAD), 1)
    eye = (rows == cols).astype(F32)
    trace = jnp.sum(jnp.sum(gram * eye, axis=1, keepdims=True), axis=0, keepdims=True)
    inv = 1.0 / (jnp.sqrt(trace) + epsilon)
    a = (gram * inv) * inv
    q = None
    for step in range(ITERS):
        m = quintic_a * eye + quintic_b * a + quintic_c * mm(a, a)
        q = m if q is None else mm(q, m)
        if step < ITERS - 1:
            a = mm(mm(m, a), m)
    return q * (inv * scale)


def kernel(
    acts_h, cot_h, kv_h, w_h, mom_h, upd_o, ig_o,
    acts_v, acts_t, acts_g, kv_v, kv_g, w_v, part, acc, rbuf, mom_v, buf,
    gram, gram_r, tot, qall, upd, out_v, gin, gout,
    ld_sem, w_sem, kv_send, kv_recv, ac_send, ac_recv, rs_send, rs_recv,
    mom_send, mom_recv, ch_send, ch_recv, ig_sem, gr_send, gr_recv,
    t_send, t_recv, q_send, q_recv, o_send, o_recv, o_sem,
):
    z = lax.axis_index("pipe")
    d = lax.axis_index("dp")
    y, x, c = lax.div(d, 8), mod4(lax.div(d, 2)), lax.rem(d, 2)
    e = 1 - c
    pg = x * e + y * c
    pr = y * e + x * c

    def chip(yy, xx, cc):
        return (z, (mod4(yy) * 4 + mod4(xx)) * 2 + cc)

    def on_g(o):
        return chip(y + o * c, x + o * e, c)

    def on_r(o):
        return chip(y + o * e, x + o * c, c)

    sib = chip(y, x, e)
    bar = pltpu.get_barrier_semaphore()

    def greet(dev):
        pl.semaphore_signal(bar, inc=1, device_id=dev, device_id_type=MESH)

    for o in FAR:
        greet(on_g(o))
        greet(chip(y + o * c, x + o * e, e))
        greet(on_r(o))
    greet(sib)

    @pl.when(z < 3)
    def _():
        greet((z + 1, d))

    def start(cp):
        cp.start()
        return cp

    ld_kv = start(pltpu.make_async_copy(kv_h, kv_v, ld_sem.at[0]))
    ld_acts = start(pltpu.make_async_copy(acts_h, acts_v, ld_sem.at[1]))
    myrow = pl.multiple_of(c * OWN, OWN)
    mycol = pl.multiple_of(c * HALF, HALF)
    sibcol = pl.multiple_of(e * HALF, HALF)
    ld_mom = start(pltpu.make_async_copy(mom_h.at[:, pl.ds(mycol, HALF)], mom_v.at[pl.ds(myrow, OWN)], ld_sem.at[2]))

    @pl.loop(0, NCH)
    def _(k):
        pltpu.make_async_copy(w_h.at[pl.ds(pl.multiple_of(k * CH, CH), CH)], w_v.at[k], w_sem.at[k]).start()

    def cols(k):
        return pl.ds(pl.multiple_of(k * CH, CH), CH)

    @pl.when(z == 3)
    def _():
        @pl.loop(0, NCH)
        def _(k):
            pltpu.make_async_copy(cot_h.at[:, cols(k)], gin.at[:, cols(k)], ch_recv.at[k]).start()

    def remote(src, dst, ssem, rsem, dev):
        return pltpu.make_async_remote_copy(src, dst, ssem, rsem, device_id=dev, device_id_type=MESH)

    pl.semaphore_wait(bar, jnp.where(z > 0, 11, 10))

    sends = []
    ld_kv.wait()
    slots = (x * 2 + c, y * 2 + c)
    for i, off in enumerate(FAR):
        for t in (0, 1):
            dev = chip(y, x + off, 0) if t == 0 else chip(y + off, x, 1)
            sends.append(start(remote(
                kv_v.at[:, t * HALF:(t + 1) * HALF],
                kv_g.at[pl.ds(pl.multiple_of(slots[t] * TOK, TOK), TOK)],
                kv_send.at[i * 2 + t], kv_recv.at[slots[t]], dev)))
    slot_own = pg * 2 + c
    slot_sib = pr * 2 + c
    own_tok = pl.ds(pl.multiple_of(slot_own * TOK, TOK), TOK)
    sib_tok = pl.ds(pl.multiple_of(slot_sib * TOK, TOK), TOK)
    start(pltpu.make_async_copy(kv_v.at[:, pl.ds(mycol, HALF)], kv_g.at[own_tok], kv_recv.at[slot_own]))
    sends.append(start(remote(
        kv_v.at[:, pl.ds(sibcol, HALF)], kv_g.at[sib_tok], kv_send.at[6], kv_recv.at[slot_sib], sib)))
    sends.append(start(remote(
        mom_h.at[:, pl.ds(sibcol, HALF)], mom_v.at[pl.ds(myrow, OWN)], mom_send.at[0], mom_recv.at[0], sib)))

    ld_acts.wait()

    @pl.loop(0, D // 512)
    def _(k):
        at = pl.multiple_of(k * 512, 512)
        acts_t[pl.ds(at, 512), :] = acts_v[:, pl.ds(at, 512)].T

    n = 0
    for o in ORDER:
        for off in FAR:
            for t in (0, 1):
                if t == 0:
                    base = (mod4(y + o) * 4 + mod4(x + off)) * ROWS
                    dev = chip(y, x + off, 0)
                else:
                    base = (mod4(y + off) * 4 + mod4(x + o)) * ROWS
                    dev = chip(y + off, x, 1)
                sends.append(start(remote(
                    acts_t.at[pl.ds(pl.multiple_of(base, ROWS), ROWS)],
                    acts_g.at[o, :, pl.ds(pl.multiple_of(slots[t] * TOK, TOK), TOK)],
                    ac_send.at[n], ac_recv.at[o, slots[t]], dev)))
                n += 1
        base_own = (mod4(y + o * e) * 4 + mod4(x + o * c)) * ROWS
        base_sib = (mod4(y + o * c) * 4 + mod4(x + o * e)) * ROWS
        start(pltpu.make_async_copy(
            acts_t.at[pl.ds(pl.multiple_of(base_own, ROWS), ROWS)], acts_g.at[o, :, own_tok], ac_recv.at[o, slot_own]))
        sends.append(start(remote(
            acts_t.at[pl.ds(pl.multiple_of(base_sib, ROWS), ROWS)], acts_g.at[o, :, sib_tok],
            ac_send.at[n], ac_recv.at[o, slot_sib], sib)))
        n += 1

    def chain(lo, hi):
        @pl.loop(lo, hi)
        def _(k):
            pltpu.make_async_copy(w_h.at[pl.ds(0, CH)], w_v.at[k], w_sem.at[k]).wait()
            own = lax.dot_general(kv_v[...], w_v[k], (((1,), (1,)), ((), ())), preferred_element_type=F32)
            pltpu.make_async_copy(cot_h.at[:, cols(k)], gin.at[:, cols(k)], ch_recv.at[k]).wait()
            gout[:, cols(k)] = (gin[:, cols(k)].astype(F32) + own).astype(BF16)

            @pl.when(z > 0)
            def _():
                remote(gout.at[:, cols(k)], gin.at[:, cols(k)], ch_send.at[k], ch_recv.at[k], (z - 1, d)).start()

            pltpu.make_async_copy(gout.at[:, cols(k)], ig_o.at[:, cols(k)], ig_sem.at[k]).start()

    at = 0
    for i, o in enumerate(ORDER):
        upto = jnp.where(z == 3, NCH, (2, 4, 7, 9)[i] + 2 * z)
        chain(at, upto)
        at = upto
        if i == 0:
            for s in range(8):
                ref = kv_g.at[s * TOK:(s + 1) * TOK]
                pltpu.make_async_copy(ref, ref, kv_recv.at[s]).wait()
        for s in range(8):
            ref = acts_g.at[o, :, s * TOK:(s + 1) * TOK]
            pltpu.make_async_copy(ref, ref, ac_recv.at[o, s]).wait()

        @pl.loop(0, HALF // 256)
        def _(j):
            span = pl.ds(pl.multiple_of(j * 256, 256), 256)
            term = jnp.dot(acts_g[o], kv_g[:, span], preferred_element_type=F32)
            if o == 0:
                acc[:, span] = term
            else:
                part[o - 1, :, span] = term.astype(BF16)

        if o != 0:
            sends.append(start(remote(part.at[o - 1], rbuf.at[o - 1], rs_send.at[o - 1], rs_recv.at[o - 1], on_r(o))))
    chain(at, NCH)

    ld_mom.wait()
    half_mom = mom_v.at[pl.ds(pl.multiple_of(e * OWN, OWN), OWN)]
    pltpu.make_async_copy(half_mom, half_mom, mom_recv.at[0]).wait()
    for o in FAR:
        ref = rbuf.at[o - 1]
        pltpu.make_async_copy(ref, ref, rs_recv.at[o - 1]).wait()

    for h in range(8):
        span = slice(h * HEAD, (h + 1) * HEAD)
        grad = acc[:, span] + rbuf[0, :, span].astype(F32) + rbuf[1, :, span].astype(F32) + rbuf[2, :, span].astype(F32)
        value = (momentum_rate * mom_v[:, span].astype(F32) + grad * (1.0 / 4096)).astype(BF16)
        buf[:, span] = value
        gram[h // 2, h % 2] = lax.dot_general(value, value, (((0,), (0,)), ((), ())), preferred_element_type=F32)

    for o in FAR:
        sends.append(start(remote(gram.at[mod4(pg + o)], gram_r.at[o - 1], gr_send.at[o - 1], gr_recv.at[o - 1], on_g(o))))
    for o in FAR:
        ref = gram_r.at[o - 1]
        pltpu.make_async_copy(ref, ref, gr_recv.at[o - 1]).wait()
    tot[pr] = gram[pg] + gram_r[0] + gram_r[1] + gram_r[2]
    for o in FAR:
        sends.append(start(remote(tot.at[pr], tot.at[pr], t_send.at[o - 1], t_recv.at[o - 1], on_r(o))))
    for o in FAR:
        ref = tot.at[mod4(pr + 4 - o)]
        pltpu.make_async_copy(ref, ref, t_recv.at[o - 1]).wait()
    scale = 0.2 * math.sqrt(max(D, HEAD))
    for h in range(2):
        qall[pg, h] = newton_schulz(tot[0, h] + tot[1, h] + tot[2, h] + tot[3, h], scale)
    for o in FAR:
        sends.append(start(remote(qall.at[pg], qall.at[pg], q_send.at[o - 1], q_recv.at[o - 1], on_g(o))))
    for o in FAR:
        ref = qall.at[mod4(pg + 4 - o)]
        pltpu.make_async_copy(ref, ref, q_recv.at[o - 1]).wait()

    for h in range(8):
        span = slice(h * HEAD, (h + 1) * HEAD)
        q = qall[h // 2, h % 2]
        high = q.astype(BF16)
        rest = q - high.astype(F32)
        mid = rest.astype(BF16)
        low = (rest - mid.astype(F32)).astype(BF16)
        value = buf[:, span]
        total = jnp.dot(value, high, preferred_element_type=F32)
        total = total + jnp.dot(value, mid, preferred_element_type=F32)
        total = total + jnp.dot(value, low, preferred_element_type=F32)
        upd[:, span] = total.astype(BF16)

    sibrow = pl.multiple_of(e * OWN, OWN)
    swap = start(remote(upd.at[pl.ds(sibrow, OWN)], out_v, o_send.at[0], o_recv.at[0], sib))
    mine = start(pltpu.make_async_copy(upd.at[pl.ds(myrow, OWN)], upd_o.at[:, pl.ds(mycol, HALF)], o_sem.at[0]))
    pltpu.make_async_copy(out_v, out_v, o_recv.at[0]).wait()
    other = start(pltpu.make_async_copy(out_v, upd_o.at[:, pl.ds(sibcol, HALF)], o_sem.at[1]))
    for cp in sends:
        cp.wait_send()
    swap.wait_send()

    @pl.loop(0, NCH)
    def _(k):
        pltpu.make_async_copy(gout.at[:, cols(k)], ig_o.at[:, cols(k)], ig_sem.at[k]).wait()

    @pl.when(z > 0)
    def _():
        @pl.loop(0, NCH)
        def _(k):
            remote(gout.at[:, cols(k)], gin.at[:, cols(k)], ch_send.at[k], ch_recv.at[k], (z - 1, d)).wait_send()

    mine.wait()
    other.wait()


def shards(acts, cotangent, kv_grads, w_kv, momentum):
    dma = pltpu.SemaphoreType.DMA
    vmem = pltpu.VMEM
    anyspec = pl.BlockSpec(memory_space=pl.ANY)
    update, grads = pl.pallas_call(
        kernel,
        out_shape=(jax.ShapeDtypeStruct((OWN, COLS), BF16), jax.ShapeDtypeStruct((TOK, D), BF16)),
        in_specs=[anyspec] * 5,
        out_specs=(anyspec, anyspec),
        scratch_shapes=[
            vmem((TOK, D), BF16), vmem((D, TOK), BF16), vmem((4, ROWS, 8 * TOK), BF16),
            vmem((TOK, COLS), BF16), vmem((8 * TOK, HALF), BF16), vmem((NCH, CH, COLS), BF16),
            vmem((3, ROWS, HALF), BF16), vmem((ROWS, HALF), F32), vmem((3, ROWS, HALF), BF16),
            vmem((ROWS, HALF), BF16), vmem((ROWS, HALF), BF16),
            vmem((4, 2, HEAD, HEAD), F32), vmem((3, 2, HEAD, HEAD), F32), vmem((4, 2, HEAD, HEAD), F32),
            vmem((4, 2, HEAD, HEAD), F32), vmem((ROWS, HALF), BF16), vmem((OWN, HALF), BF16),
            vmem((TOK, D), BF16), vmem((TOK, D), BF16),
            dma((3,)), dma((NCH,)), dma((7,)), dma((8,)), dma((28,)), dma((4, 8)), dma((3,)), dma((3,)),
            dma((1,)), dma((1,)), dma((NCH,)), dma((NCH,)), dma((NCH,)), dma((3,)), dma((3,)),
            dma((3,)), dma((3,)), dma((3,)), dma((3,)), dma((1,)), dma((1,)), dma((2,)),
        ],
        name="muon_back",
        compiler_params=pltpu.CompilerParams(
            collective_id=0, has_side_effects=True, vmem_limit_bytes=60 * 1024 * 1024
        ),
    )(acts[0], cotangent, kv_grads[0], w_kv[0], momentum[0])
    return update[None], grads[None]


def solution(mesh):
    in_specs = (
        P("pipe", "dp", None),
        P("dp", None),
        P("pipe", "dp", None),
        P("pipe", None, None),
        P("pipe", "dp", None),
    )
    out_specs = (P("pipe", "dp", None), P("pipe", "dp", None))
    return jax.shard_map(shards, mesh=mesh, in_specs=in_specs, out_specs=out_specs, check_vma=False)
```

```python
import functools
import math

import jax
import jax.numpy as jnp
from jax import lax
from jax.experimental import pallas as pl
from jax.experimental.pallas import tpu as pltpu
from jax.sharding import PartitionSpec as P

MESH = pl.DeviceIdType.MESH
F32 = jnp.float32
BF16 = jnp.bfloat16
HEAD = 128
ITERS = 5
TOK = 128
D = 5120
COLS = 2048
HALF = 1024
QC = 512
ROWS = 320
OWN = 160
CH = 256
NCH = D // CH
FAR = (2, 1, 3)

momentum_rate = 0.95
quintic_a = 3.4445
quintic_b = -4.775
quintic_c = 2.0315
epsilon = 1e-07


def mod4(v):
    return lax.rem(v, 4)


def split(a):
    high = a.astype(BF16)
    rest = a - high.astype(F32)
    mid = rest.astype(BF16)
    return high, mid, (rest - mid.astype(F32)).astype(BF16)


def mm(sa, sb):
    a1, a2, a3 = sa
    b1, b2, b3 = sb
    right = jnp.concatenate([jnp.concatenate([b2, b3], 1), jnp.concatenate([b1, b2], 1)], 0)
    small = jnp.dot(jnp.concatenate([a1, a2], 1), right, preferred_element_type=F32)
    big = jnp.dot(jnp.concatenate([a1, a3], 1), jnp.concatenate([b1, b1], 0), preferred_element_type=F32)
    return big + (small[:, :HEAD] + small[:, HEAD:])


def newton_schulz(gram, scale):
    rows = lax.broadcasted_iota(jnp.int32, (HEAD, HEAD), 0)
    cols = lax.broadcasted_iota(jnp.int32, (HEAD, HEAD), 1)
    eye = (rows == cols).astype(F32)
    trace = jnp.sum(jnp.sum(gram * eye, axis=1, keepdims=True), axis=0, keepdims=True)
    inv = 1.0 / (jnp.sqrt(trace) + epsilon)
    a = (gram * inv) * inv
    q = None
    for step in range(ITERS):
        sa = split(a)
        m = quintic_a * eye + quintic_b * a + quintic_c * mm(sa, sa)
        sm = split(m)
        q = m if q is None else mm(split(q), sm)
        if step < ITERS - 1:
            a = mm(split(mm(sm, sa)), sm)
    return q * (inv * scale)


def kernel(
    acts_h, cot_h, kv_h, w_h, mom_h, upd_o, ig_o,
    acts_v, acts_t, acts_g, kv_v, kv_g, w_v, part, trans, acc, rbuf, mom_v, buf,
    gram, gram_r, tot, qall, upd, out_v, gin, gout,
    ld_sem, w_sem, send_sem, kv_recv, kvf_recv, ac_recv, tr_recv, rs_recv,
    mom_recv, ch_send, ch_recv, ig_sem, gr_recv, t_recv, q_recv, o_recv, o_sem,
):
    z = lax.axis_index("pipe")
    d = lax.axis_index("dp")
    y, x, c = lax.div(d, 8), mod4(lax.div(d, 2)), lax.rem(d, 2)
    e = 1 - c
    pg = x * e + y * c
    pr = y * e + x * c

    def chip(yy, xx, cc):
        return (z, (mod4(yy) * 4 + mod4(xx)) * 2 + cc)

    def on_g(o):
        return chip(y + o * c, x + o * e, c)

    def on_r(o):
        return chip(y + o * e, x + o * c, c)

    sib = chip(y, x, e)
    bar = pltpu.get_barrier_semaphore()

    def greet(dev):
        pl.semaphore_signal(bar, inc=1, device_id=dev, device_id_type=MESH)

    for o in FAR:
        greet(on_g(o))
        greet(chip(y + o * c, x + o * e, e))
        greet(on_r(o))
    greet(sib)

    @pl.when(z < 3)
    def _():
        greet((z + 1, d))

    def start(cp):
        cp.start()
        return cp

    def remote(src, dst, ssem, rsem, dev):
        return pltpu.make_async_remote_copy(src, dst, ssem, rsem, device_id=dev, device_id_type=MESH)

    sends = []

    def send(src, dst, rsem, dev):
        sends.append(start(remote(src, dst, send_sem.at[len(sends)], rsem, dev)))

    def wait(ref, sem):
        pltpu.make_async_copy(ref, ref, sem).wait()

    def cols(k):
        return pl.ds(pl.multiple_of(k * CH, CH), CH)

    ld_kv = start(pltpu.make_async_copy(kv_h, kv_v, ld_sem.at[0]))
    ld_acts = start(pltpu.make_async_copy(acts_h, acts_v, ld_sem.at[1]))
    myrow = pl.multiple_of(c * OWN, OWN)
    sibrow = pl.multiple_of(e * OWN, OWN)
    mycol = pl.multiple_of(c * HALF, HALF)
    sibcol = pl.multiple_of(e * HALF, HALF)
    ld_mom = start(pltpu.make_async_copy(mom_h.at[:, pl.ds(mycol, HALF)], mom_v.at[pl.ds(myrow, OWN)], ld_sem.at[2]))

    @pl.loop(0, NCH)
    def _(k):
        pltpu.make_async_copy(w_h.at[pl.ds(pl.multiple_of(k * CH, CH), CH)], w_v.at[k], w_sem.at[k]).start()

    @pl.when(z == 3)
    def _():
        @pl.loop(0, NCH)
        def _(k):
            pltpu.make_async_copy(cot_h.at[:, cols(k)], gin.at[:, cols(k)], ch_recv.at[k]).start()

    pl.semaphore_wait(bar, jnp.where(z > 0, 11, 10))

    def toks(slot, first=0, count=TOK):
        return pl.ds(pl.multiple_of(slot * TOK + first, count), count)

    slots = (x * 2 + c, y * 2 + c)
    slot_own = pg * 2 + c
    slot_sib = pr * 2 + c
    ld_kv.wait()
    for q in range(2):
        for off in (1, 3):
            for t in (0, 1):
                dev = chip(y, x + off, 0) if t == 0 else chip(y + off, x, 1)
                at = t * HALF + q * QC
                send(kv_v.at[:, at:at + QC], kv_g.at[q, toks(slots[t])], kv_recv.at[q, off, c], dev)
        own_at = pl.ds(pl.multiple_of(mycol + q * QC, QC), QC)
        sib_at = pl.ds(pl.multiple_of(sibcol + q * QC, QC), QC)
        start(pltpu.make_async_copy(kv_v.at[:, own_at], kv_g.at[q, toks(slot_own)], kv_recv.at[q, 0, c]))
        send(kv_v.at[:, sib_at], kv_g.at[q, toks(slot_sib)], kv_recv.at[q, 0, c], sib)

    def chain(lo, hi):
        @pl.loop(lo, hi)
        def _(k):
            wait(w_v.at[k], w_sem.at[k])
            own = lax.dot_general(kv_v[...], w_v[k], (((1,), (1,)), ((), ())), preferred_element_type=F32)
            wait(gin.at[:, cols(k)], ch_recv.at[k])
            gout[:, cols(k)] = (gin[:, cols(k)].astype(F32) + own).astype(BF16)

            @pl.when(z > 0)
            def _():
                remote(gout.at[:, cols(k)], gin.at[:, cols(k)], ch_send.at[k], ch_recv.at[k], (z - 1, d)).start()

            pltpu.make_async_copy(gout.at[:, cols(k)], ig_o.at[:, cols(k)], ig_sem.at[k]).start()

    def steps(base, last):
        return jnp.where(z == 3, last, jnp.maximum(base + 2 * z, 0))

    at0 = steps(-100, 6)
    chain(0, at0)

    send(mom_h.at[:, pl.ds(sibcol, HALF)], mom_v.at[pl.ds(myrow, OWN)], mom_recv.at[0], sib)
    ld_acts.wait()

    @pl.loop(0, D // 512)
    def _(k):
        at = pl.multiple_of(k * 512, 512)
        acts_t[pl.ds(at, 512), :] = acts_v[:, pl.ds(at, 512)].T

    def send_acts(o):
        for off in FAR:
            for t in (0, 1):
                if t == 0:
                    base = (mod4(y + o) * 4 + mod4(x + off)) * ROWS
                    dev = chip(y, x + off, 0)
                else:
                    base = (mod4(y + off) * 4 + mod4(x + o)) * ROWS
                    dev = chip(y + off, x, 1)
                send(acts_t.at[pl.ds(pl.multiple_of(base, ROWS), ROWS)],
                     acts_g.at[o, :, toks(slots[t])], ac_recv.at[o, off, c], dev)
        base_own = (mod4(y + o * e) * 4 + mod4(x + o * c)) * ROWS
        base_sib = (mod4(y + o * c) * 4 + mod4(x + o * e)) * ROWS
        start(pltpu.make_async_copy(
            acts_t.at[pl.ds(pl.multiple_of(base_own, ROWS), ROWS)], acts_g.at[o, :, toks(slot_own)], ac_recv.at[o, 0, c]))
        send(acts_t.at[pl.ds(pl.multiple_of(base_sib, ROWS), ROWS)],
             acts_g.at[o, :, toks(slot_sib)], ac_recv.at[o, 0, c], sib)

    send_acts(2)
    send_acts(1)
    at1 = steps(0, 12)
    chain(at0, at1)
    for q in range(2):
        for off in (1, 3, 0):
            for cc in (0, 1):
                wait(kv_g.at[q, toks(mod4(pg + 4 - off) * 2 + cc)], kv_recv.at[q, off, cc])
                if off:
                    piece = kv_g.at[q, toks(mod4(pg + 4 - off) * 2 + cc, 0 if off == 1 else 64, 64)]
                    send(piece, piece, kvf_recv.at[q, off // 2, cc], on_g(off))
    send_acts(3)
    send_acts(0)
    at2 = steps(6, NCH)
    chain(at1, at2)
    for q in range(2):
        for half in range(2):
            for cc in (0, 1):
                wait(kv_g.at[q, toks(mod4(pg + 2) * 2 + cc, half * 64, 64)], kvf_recv.at[q, half, cc])

    def wait_acts(o):
        for off in range(4):
            for cc in (0, 1):
                wait(acts_g.at[o, :, toks(mod4(pg + 4 - off) * 2 + cc)], ac_recv.at[o, off, cc])

    def block(o, q):
        @pl.loop(0, QC // 256)
        def _(j):
            span = pl.ds(pl.multiple_of(j * 256, 256), 256)
            term = jnp.dot(acts_g[o], kv_g[q, :, span], preferred_element_type=F32)
            if o == 0:
                acc[q, :, span] = term
            elif o == 2:
                part[q, o - 1, :, span] = term.astype(BF16)
            elif o == 1:
                part[q, o - 1, :OWN, span] = (term[:OWN] + trans[q, 0, :, span].astype(F32)).astype(BF16)
                part[q, o - 1, OWN:, span] = term[OWN:].astype(BF16)
            else:
                part[q, o - 1, :OWN, span] = term[:OWN].astype(BF16)
                part[q, o - 1, OWN:, span] = (term[OWN:] + trans[q, 1, :, span].astype(F32)).astype(BF16)

    wait_acts(2)
    for q in range(2):
        block(2, q)
        send(part.at[q, 1, :OWN], trans.at[q, 0], tr_recv.at[q, 0], on_r(1))
        send(part.at[q, 1, OWN:], trans.at[q, 1], tr_recv.at[q, 1], on_r(3))
    at3 = steps(10, NCH)
    chain(at2, at3)
    wait_acts(1)
    wait_acts(3)
    for q in range(2):
        for o in (1, 3):
            wait(trans.at[q, o // 2], tr_recv.at[q, o // 2])
            block(o, q)
            send(part.at[q, o - 1], rbuf.at[q, o // 2], rs_recv.at[q, o // 2], on_r(o))
    wait_acts(0)
    for q in range(2):
        block(0, q)
    at4 = steps(16, NCH)
    at4 = jnp.minimum(at4, NCH)
    chain(at3, at4)

    ld_mom.wait()
    wait(mom_v.at[pl.ds(sibrow, OWN)], mom_recv.at[0])

    def gram_of(q):
        for s in range(2):
            wait(rbuf.at[q, s], rs_recv.at[q, s])
        for h in range(4):
            span = slice(h * HEAD, (h + 1) * HEAD)
            grad = acc[q, :, span] + rbuf[q, 0, :, span].astype(F32) + rbuf[q, 1, :, span].astype(F32)
            mom = mom_v[:, q * QC + h * HEAD:q * QC + (h + 1) * HEAD].astype(F32)
            value = (momentum_rate * mom + grad * (1.0 / 4096)).astype(BF16)
            buf[q, :, span] = value
            gram[q, h] = lax.dot_general(value, value, (((0,), (0,)), ((), ())), preferred_element_type=F32)
        for o in FAR:
            send(gram.at[q, mod4(pg + o)], gram_r.at[q, o - 1], gr_recv.at[q, o - 1], on_g(o))

    def combine(q):
        for o in FAR:
            wait(gram_r.at[q, o - 1], gr_recv.at[q, o - 1])
        tot[q, pr] = gram[q, pg] + gram_r[q, 0] + gram_r[q, 1] + gram_r[q, 2]
        for o in FAR:
            send(tot.at[q, pr], tot.at[q, pr], t_recv.at[q, o - 1], on_r(o))

    def iterate(q):
        for o in FAR:
            wait(tot.at[q, mod4(pr + 4 - o)], t_recv.at[q, o - 1])
        scale = 0.2 * math.sqrt(max(D, HEAD))
        qall[q, pg] = newton_schulz((tot[q, 0] + tot[q, 1]) + (tot[q, 2] + tot[q, 3]), scale)
        for o in FAR:
            send(qall.at[q, pg], qall.at[q, pg], q_recv.at[q, o - 1], on_g(o))

    outs = []

    def finish(q):
        for o in FAR:
            wait(qall.at[q, mod4(pg + 4 - o)], q_recv.at[q, o - 1])
        for h in range(4):
            span = slice(h * HEAD, (h + 1) * HEAD)
            high, mid, low = split(qall[q, h])
            value = buf[q, :, span]
            total = jnp.dot(value, low, preferred_element_type=F32) + jnp.dot(value, mid, preferred_element_type=F32)
            upd[q, :, span] = (total + jnp.dot(value, high, preferred_element_type=F32)).astype(BF16)
        send(upd.at[q, pl.ds(sibrow, OWN)], out_v.at[q], o_recv.at[q], sib)
        place = pl.ds(pl.multiple_of(mycol + q * QC, QC), QC)
        outs.append(start(pltpu.make_async_copy(upd.at[q, pl.ds(myrow, OWN)], upd_o.at[:, place], o_sem.at[q])))

    gram_of(0)
    chain(at4, NCH)
    combine(0)
    gram_of(1)
    iterate(0)
    combine(1)
    finish(0)
    iterate(1)
    finish(1)
    for q in range(2):
        wait(out_v.at[q], o_recv.at[q])
        place = pl.ds(pl.multiple_of(sibcol + q * QC, QC), QC)
        outs.append(start(pltpu.make_async_copy(out_v.at[q], upd_o.at[:, place], o_sem.at[2 + q])))
    for cp in sends:
        cp.wait_send()

    @pl.loop(0, NCH)
    def _(k):
        wait(gout.at[:, cols(k)], ig_sem.at[k])

    @pl.when(z > 0)
    def _():
        @pl.loop(0, NCH)
        def _(k):
            remote(gout.at[:, cols(k)], gin.at[:, cols(k)], ch_send.at[k], ch_recv.at[k], (z - 1, d)).wait_send()

    for cp in outs:
        cp.wait()


def shards(acts, cotangent, kv_grads, w_kv, momentum):
    dma = pltpu.SemaphoreType.DMA
    vmem = pltpu.VMEM
    anyspec = pl.BlockSpec(memory_space=pl.ANY)
    update, grads = pl.pallas_call(
        kernel,
        out_shape=(jax.ShapeDtypeStruct((OWN, COLS), BF16), jax.ShapeDtypeStruct((TOK, D), BF16)),
        in_specs=[anyspec] * 5,
        out_specs=(anyspec, anyspec),
        scratch_shapes=[
            vmem((TOK, D), BF16), vmem((D, TOK), BF16), vmem((4, ROWS, 8 * TOK), BF16),
            vmem((TOK, COLS), BF16), vmem((2, 8 * TOK, QC), BF16), vmem((NCH, CH, COLS), BF16),
            vmem((2, 3, ROWS, QC), BF16), vmem((2, 2, OWN, QC), BF16), vmem((2, ROWS, QC), F32),
            vmem((2, 2, ROWS, QC), BF16), vmem((ROWS, HALF), BF16), vmem((2, ROWS, QC), BF16),
            vmem((2, 4, HEAD, HEAD), F32), vmem((2, 3, HEAD, HEAD), F32), vmem((2, 4, HEAD, HEAD), F32),
            vmem((2, 4, HEAD, HEAD), F32), vmem((2, ROWS, QC), BF16), vmem((2, OWN, QC), BF16),
            vmem((TOK, D), BF16), vmem((TOK, D), BF16),
            dma((3,)), dma((NCH,)), dma((92,)), dma((2, 4, 2)), dma((2, 2, 2)), dma((4, 4, 2)),
            dma((2, 2)), dma((2, 2)), dma((1,)), dma((NCH,)), dma((NCH,)), dma((NCH,)), dma((2, 3)),
            dma((2, 3)), dma((2, 3)), dma((2,)), dma((4,)),
        ],
        name="muon_back",
        compiler_params=pltpu.CompilerParams(
            collective_id=0, has_side_effects=True, vmem_limit_bytes=60 * 1024 * 1024
        ),
    )(acts[0], cotangent, kv_grads[0], w_kv[0], momentum[0])
    return update[None], grads[None]


def solution(mesh):
    in_specs = (
        P("pipe", "dp", None),
        P("dp", None),
        P("pipe", "dp", None),
        P("pipe", None, None),
        P("pipe", "dp", None),
    )
    out_specs = (P("pipe", "dp", None), P("pipe", "dp", None))
    return jax.shard_map(shards, mesh=mesh, in_specs=in_specs, out_specs=out_specs, check_vma=False)
```

```python
import functools
import math

import jax
import jax.numpy as jnp
from jax import lax
from jax.experimental import pallas as pl
from jax.experimental.pallas import tpu as pltpu
from jax.sharding import PartitionSpec as P

MESH = pl.DeviceIdType.MESH
F32 = jnp.float32
BF16 = jnp.bfloat16
HEAD = 128
ITERS = 5
TOK = 128
D = 5120
COLS = 2048
HALF = 1024
QC = 512
ROWS = 320
OWN = 160
CH = 256
NCH = D // CH
FAR = (2, 1, 3)
PLAN = (
    ((0, 0, 0, 6), (0, 0, 0, 6)),
    ((10, 10, 4, 12), (0, 0, 1, 12)),
    ((20, 20, 14, 20), (1, 4, 7, 20)),
    ((20, 20, 20, 20), (5, 8, 12, 20)),
    ((20, 20, 20, 20), (9, 12, 15, 20)),
    ((20, 20, 20, 20), (11, 14, 17, 20)),
    ((20, 20, 20, 20), (15, 18, 20, 20)),
    ((20, 20, 20, 20), (18, 20, 20, 20)),
    ((20, 20, 20, 20), (20, 20, 20, 20)),
)

momentum_rate = 0.95
quintic_a = 3.4445
quintic_b = -4.775
quintic_c = 2.0315
epsilon = 1e-07


def mod4(v):
    return lax.rem(v, 4)


def split(a):
    high = a.astype(BF16)
    rest = a - high.astype(F32)
    mid = rest.astype(BF16)
    return high, mid, (rest - mid.astype(F32)).astype(BF16)


def mm(sa, sb):
    a1, a2, a3 = sa
    b1, b2, b3 = sb
    right = jnp.concatenate([jnp.concatenate([b2, b3], 1), jnp.concatenate([b1, b2], 1)], 0)
    small = jnp.dot(jnp.concatenate([a1, a2], 1), right, preferred_element_type=F32)
    big = jnp.dot(jnp.concatenate([a1, a3], 1), jnp.concatenate([b1, b1], 0), preferred_element_type=F32)
    return big + (small[:, :HEAD] + small[:, HEAD:])


def newton_schulz(gram, scale):
    rows = lax.broadcasted_iota(jnp.int32, (HEAD, HEAD), 0)
    cols = lax.broadcasted_iota(jnp.int32, (HEAD, HEAD), 1)
    eye = (rows == cols).astype(F32)
    trace = jnp.sum(jnp.sum(gram * eye, axis=1, keepdims=True), axis=0, keepdims=True)
    inv = 1.0 / (jnp.sqrt(trace) + epsilon)
    a = (gram * inv) * inv
    q = None
    for step in range(ITERS):
        sa = split(a)
        m = quintic_a * eye + quintic_b * a + quintic_c * mm(sa, sa)
        sm = split(m)
        q = m if q is None else mm(split(q), sm)
        if step < ITERS - 1:
            a = mm(split(mm(sm, sa)), sm)
    return q * (inv * scale)


def kernel(
    acts_h, cot_h, kv_h, w_h, mom_h, upd_o, ig_o,
    acts_v, acts_t, acts_g, kv_v, kv_g, w_v, part, trans, acc, rbuf, mom_v, buf,
    gram, gram_r, tot, qall, upd, out_v, gin, gout, own_v,
    ld_sem, w_sem, send_sem, kv_recv, kvf_recv, ac_recv, tr_recv, rs_recv,
    mom_recv, ch_send, ch_recv, ig_sem, gr_recv, t_recv, q_recv, o_recv, o_sem,
):
    z = lax.axis_index("pipe")
    d = lax.axis_index("dp")
    y, x, c = lax.div(d, 8), mod4(lax.div(d, 2)), lax.rem(d, 2)
    e = 1 - c
    pg = x * e + y * c
    pr = y * e + x * c

    def chip(yy, xx, cc):
        return (z, (mod4(yy) * 4 + mod4(xx)) * 2 + cc)

    def on_g(o):
        return chip(y + o * c, x + o * e, c)

    def on_r(o):
        return chip(y + o * e, x + o * c, c)

    sib = chip(y, x, e)
    bar = pltpu.get_barrier_semaphore()

    def greet(dev):
        pl.semaphore_signal(bar, inc=1, device_id=dev, device_id_type=MESH)

    for o in FAR:
        greet(on_g(o))
        greet(chip(y + o * c, x + o * e, e))
        greet(on_r(o))
    greet(sib)

    @pl.when(z < 3)
    def _():
        greet((z + 1, d))

    def start(cp):
        cp.start()
        return cp

    def remote(src, dst, ssem, rsem, dev):
        return pltpu.make_async_remote_copy(src, dst, ssem, rsem, device_id=dev, device_id_type=MESH)

    sends = []

    def send(src, dst, rsem, dev):
        sends.append(start(remote(src, dst, send_sem.at[len(sends)], rsem, dev)))

    def wait(ref, sem):
        pltpu.make_async_copy(ref, ref, sem).wait()

    def cols(k):
        return pl.ds(pl.multiple_of(k * CH, CH), CH)

    ld_kv = start(pltpu.make_async_copy(kv_h, kv_v, ld_sem.at[0]))
    ld_acts = start(pltpu.make_async_copy(acts_h, acts_v, ld_sem.at[1]))
    myrow = pl.multiple_of(c * OWN, OWN)
    sibrow = pl.multiple_of(e * OWN, OWN)
    mycol = pl.multiple_of(c * HALF, HALF)
    sibcol = pl.multiple_of(e * HALF, HALF)
    ld_mom = start(pltpu.make_async_copy(mom_h.at[:, pl.ds(mycol, HALF)], mom_v.at[pl.ds(myrow, OWN)], ld_sem.at[2]))

    @pl.loop(0, NCH)
    def _(k):
        pltpu.make_async_copy(w_h.at[pl.ds(pl.multiple_of(k * CH, CH), CH)], w_v.at[k], w_sem.at[k]).start()

    @pl.when(z == 3)
    def _():
        @pl.loop(0, NCH)
        def _(k):
            pltpu.make_async_copy(cot_h.at[:, cols(k)], gin.at[k], ch_recv.at[k]).start()

    pl.semaphore_wait(bar, jnp.where(z > 0, 11, 10))

    def toks(slot, first=0, count=TOK):
        return pl.ds(pl.multiple_of(slot * TOK + first, count), count)

    slots = (x * 2 + c, y * 2 + c)
    slot_own = pg * 2 + c
    slot_sib = pr * 2 + c
    ld_kv.wait()
    for q in range(2):
        for off in (1, 3):
            for t in (0, 1):
                dev = chip(y, x + off, 0) if t == 0 else chip(y + off, x, 1)
                at = t * HALF + q * QC
                send(kv_v.at[:, at:at + QC], kv_g.at[q, toks(slots[t])], kv_recv.at[q, off, c], dev)
        own_at = pl.ds(pl.multiple_of(mycol + q * QC, QC), QC)
        sib_at = pl.ds(pl.multiple_of(sibcol + q * QC, QC), QC)
        start(pltpu.make_async_copy(kv_v.at[:, own_at], kv_g.at[q, toks(slot_own)], kv_recv.at[q, 0, c]))
        send(kv_v.at[:, sib_at], kv_g.at[q, toks(slot_sib)], kv_recv.at[q, 0, c], sib)

    def product(k):
        wait(w_v.at[k], w_sem.at[k])
        own_v[k] = lax.dot_general(kv_v[...], w_v[k], (((1,), (1,)), ((), ())), preferred_element_type=F32)

    def relay(k):
        wait(gin.at[k], ch_recv.at[k])
        gout[k] = (gin[k].astype(F32) + own_v[k]).astype(BF16)

        @pl.when(z > 0)
        def _():
            remote(gout.at[k], gin.at[k], ch_send.at[k], ch_recv.at[k], (z - 1, d)).start()

        pltpu.make_async_copy(gout.at[k], ig_o.at[:, cols(k)], ig_sem.at[k]).start()

    done = [0, 0]

    def chain(ahead, upto):
        ready, sent = (jnp.where(z == 0, a[0], jnp.where(z == 1, a[1], jnp.where(z == 2, a[2], a[3]))) for a in (ahead, upto))

        @pl.loop(0, jnp.maximum(ready - done[0], sent - done[1]))
        def _(n):
            @pl.when(done[0] + n < ready)
            def _():
                product(done[0] + n)

            @pl.when(done[1] + n < sent)
            def _():
                relay(done[1] + n)

        done[:] = [ready, sent]

    chain(*PLAN[0])

    send(mom_h.at[:, pl.ds(sibcol, HALF)], mom_v.at[pl.ds(myrow, OWN)], mom_recv.at[0], sib)
    ld_acts.wait()

    @pl.loop(0, D // 512)
    def _(k):
        at = pl.multiple_of(k * 512, 512)
        acts_t[pl.ds(at, 512), :] = acts_v[:, pl.ds(at, 512)].T

    def send_acts(o):
        for off in FAR:
            for t in (0, 1):
                if t == 0:
                    base = (mod4(y + o) * 4 + mod4(x + off)) * ROWS
                    dev = chip(y, x + off, 0)
                else:
                    base = (mod4(y + off) * 4 + mod4(x + o)) * ROWS
                    dev = chip(y + off, x, 1)
                send(acts_t.at[pl.ds(pl.multiple_of(base, ROWS), ROWS)],
                     acts_g.at[o, :, toks(slots[t])], ac_recv.at[o, off, c], dev)
        base_own = (mod4(y + o * e) * 4 + mod4(x + o * c)) * ROWS
        base_sib = (mod4(y + o * c) * 4 + mod4(x + o * e)) * ROWS
        start(pltpu.make_async_copy(
            acts_t.at[pl.ds(pl.multiple_of(base_own, ROWS), ROWS)], acts_g.at[o, :, toks(slot_own)], ac_recv.at[o, 0, c]))
        send(acts_t.at[pl.ds(pl.multiple_of(base_sib, ROWS), ROWS)],
             acts_g.at[o, :, toks(slot_sib)], ac_recv.at[o, 0, c], sib)

    send_acts(2)
    chain(*PLAN[1])
    for q in range(2):
        for off in (1, 3, 0):
            for cc in (0, 1):
                wait(kv_g.at[q, toks(mod4(pg + 4 - off) * 2 + cc)], kv_recv.at[q, off, cc])
                if off:
                    piece = kv_g.at[q, toks(mod4(pg + 4 - off) * 2 + cc, 0 if off == 1 else 64, 64)]
                    send(piece, piece, kvf_recv.at[q, off // 2, cc], on_g(off))
    send_acts(1)
    send_acts(3)
    chain(*PLAN[2])
    for q in range(2):
        for half in range(2):
            for cc in (0, 1):
                wait(kv_g.at[q, toks(mod4(pg + 2) * 2 + cc, half * 64, 64)], kvf_recv.at[q, half, cc])

    def wait_acts(o):
        for off in range(4):
            for cc in (0, 1):
                wait(acts_g.at[o, :, toks(mod4(pg + 4 - off) * 2 + cc)], ac_recv.at[o, off, cc])

    def block(o, q):
        @pl.loop(0, QC // 256)
        def _(j):
            span = pl.ds(pl.multiple_of(j * 256, 256), 256)
            term = jnp.dot(acts_g[o], kv_g[q, :, span], preferred_element_type=F32)
            if o == 0:
                acc[q, :, span] = term
            elif o == 2:
                part[q, o - 1, :, span] = term.astype(BF16)
            elif o == 1:
                part[q, o - 1, :OWN, span] = (term[:OWN] + trans[q, 0, :, span].astype(F32)).astype(BF16)
                part[q, o - 1, OWN:, span] = term[OWN:].astype(BF16)
            else:
                part[q, o - 1, :OWN, span] = term[:OWN].astype(BF16)
                part[q, o - 1, OWN:, span] = (term[OWN:] + trans[q, 1, :, span].astype(F32)).astype(BF16)

    wait_acts(2)
    for q in range(2):
        block(2, q)
        send(part.at[q, 1, :OWN], trans.at[q, 0], tr_recv.at[q, 0], on_r(1))
        send(part.at[q, 1, OWN:], trans.at[q, 1], tr_recv.at[q, 1], on_r(3))
    send_acts(0)
    chain(*PLAN[3])
    wait_acts(1)
    wait_acts(3)
    for q in range(2):
        for o in (1, 3):
            wait(trans.at[q, o // 2], tr_recv.at[q, o // 2])
            block(o, q)
            send(part.at[q, o - 1], rbuf.at[q, o // 2], rs_recv.at[q, o // 2], on_r(o))
    wait_acts(0)
    for q in range(2):
        block(0, q)
    chain(*PLAN[4])

    ld_mom.wait()
    wait(mom_v.at[pl.ds(sibrow, OWN)], mom_recv.at[0])

    def gram_of(q):
        for s in range(2):
            wait(rbuf.at[q, s], rs_recv.at[q, s])
        for h in range(4):
            span = slice(h * HEAD, (h + 1) * HEAD)
            grad = acc[q, :, span] + rbuf[q, 0, :, span].astype(F32) + rbuf[q, 1, :, span].astype(F32)
            mom = mom_v[:, q * QC + h * HEAD:q * QC + (h + 1) * HEAD].astype(F32)
            value = (momentum_rate * mom + grad * (1.0 / 4096)).astype(BF16)
            buf[q, :, span] = value
            gram[q, h] = lax.dot_general(value, value, (((0,), (0,)), ((), ())), preferred_element_type=F32)
        for o in FAR:
            send(gram.at[q, mod4(pg + o)], gram_r.at[q, o - 1], gr_recv.at[q, o - 1], on_g(o))

    def combine(q):
        for o in FAR:
            wait(gram_r.at[q, o - 1], gr_recv.at[q, o - 1])
        tot[q, pr] = gram[q, pg] + gram_r[q, 0] + gram_r[q, 1] + gram_r[q, 2]
        for o in FAR:
            send(tot.at[q, pr], tot.at[q, pr], t_recv.at[q, o - 1], on_r(o))

    def iterate(q):
        for o in FAR:
            wait(tot.at[q, mod4(pr + 4 - o)], t_recv.at[q, o - 1])
        scale = 0.2 * math.sqrt(max(D, HEAD))
        qall[q, pg] = newton_schulz((tot[q, 0] + tot[q, 1]) + (tot[q, 2] + tot[q, 3]), scale)
        for o in FAR:
            send(qall.at[q, pg], qall.at[q, pg], q_recv.at[q, o - 1], on_g(o))

    outs = []

    def finish(q):
        for o in FAR:
            wait(qall.at[q, mod4(pg + 4 - o)], q_recv.at[q, o - 1])
        for h in range(4):
            span = slice(h * HEAD, (h + 1) * HEAD)
            high, mid, low = split(qall[q, h])
            value = buf[q, :, span]
            total = jnp.dot(value, low, preferred_element_type=F32) + jnp.dot(value, mid, preferred_element_type=F32)
            upd[q, :, span] = (total + jnp.dot(value, high, preferred_element_type=F32)).astype(BF16)
        send(upd.at[q, pl.ds(sibrow, OWN)], out_v.at[q], o_recv.at[q], sib)
        place = pl.ds(pl.multiple_of(mycol + q * QC, QC), QC)
        outs.append(start(pltpu.make_async_copy(upd.at[q, pl.ds(myrow, OWN)], upd_o.at[:, place], o_sem.at[q])))

    gram_of(0)
    chain(*PLAN[5])
    combine(0)
    gram_of(1)
    chain(*PLAN[6])
    combine(1)
    iterate(0)
    chain(*PLAN[7])
    iterate(1)
    chain(*PLAN[8])
    finish(0)
    finish(1)
    for q in range(2):
        wait(out_v.at[q], o_recv.at[q])
        place = pl.ds(pl.multiple_of(sibcol + q * QC, QC), QC)
        outs.append(start(pltpu.make_async_copy(out_v.at[q], upd_o.at[:, place], o_sem.at[2 + q])))
    for cp in sends:
        cp.wait_send()

    @pl.loop(0, NCH)
    def _(k):
        wait(gout.at[k], ig_sem.at[k])

    @pl.when(z > 0)
    def _():
        @pl.loop(0, NCH)
        def _(k):
            remote(gout.at[k], gin.at[k], ch_send.at[k], ch_recv.at[k], (z - 1, d)).wait_send()

    for cp in outs:
        cp.wait()


def shards(acts, cotangent, kv_grads, w_kv, momentum):
    dma = pltpu.SemaphoreType.DMA
    vmem = pltpu.VMEM
    anyspec = pl.BlockSpec(memory_space=pl.ANY)
    update, grads = pl.pallas_call(
        kernel,
        out_shape=(jax.ShapeDtypeStruct((OWN, COLS), BF16), jax.ShapeDtypeStruct((TOK, D), BF16)),
        in_specs=[anyspec] * 5,
        out_specs=(anyspec, anyspec),
        scratch_shapes=[
            vmem((TOK, D), BF16), vmem((D, TOK), BF16), vmem((4, ROWS, 8 * TOK), BF16),
            vmem((TOK, COLS), BF16), vmem((2, 8 * TOK, QC), BF16), vmem((NCH, CH, COLS), BF16),
            vmem((2, 3, ROWS, QC), BF16), vmem((2, 2, OWN, QC), BF16), vmem((2, ROWS, QC), F32),
            vmem((2, 2, ROWS, QC), BF16), vmem((ROWS, HALF), BF16), vmem((2, ROWS, QC), BF16),
            vmem((2, 4, HEAD, HEAD), F32), vmem((2, 3, HEAD, HEAD), F32), vmem((2, 4, HEAD, HEAD), F32),
            vmem((2, 4, HEAD, HEAD), F32), vmem((2, ROWS, QC), BF16), vmem((2, OWN, QC), BF16),
            vmem((NCH, TOK, CH), BF16), vmem((NCH, TOK, CH), BF16), vmem((NCH, TOK, CH), F32),
            dma((3,)), dma((NCH,)), dma((92,)), dma((2, 4, 2)), dma((2, 2, 2)), dma((4, 4, 2)),
            dma((2, 2)), dma((2, 2)), dma((1,)), dma((NCH,)), dma((NCH,)), dma((NCH,)), dma((2, 3)),
            dma((2, 3)), dma((2, 3)), dma((2,)), dma((4,)),
        ],
        name="muon_back",
        compiler_params=pltpu.CompilerParams(
            collective_id=0, has_side_effects=True, vmem_limit_bytes=60 * 1024 * 1024
        ),
    )(acts[0], cotangent, kv_grads[0], w_kv[0], momentum[0])
    return update[None], grads[None]


def solution(mesh):
    in_specs = (
        P("pipe", "dp", None),
        P("dp", None),
        P("pipe", "dp", None),
        P("pipe", None, None),
        P("pipe", "dp", None),
    )
    out_specs = (P("pipe", "dp", None), P("pipe", "dp", None))
    return jax.shard_map(shards, mesh=mesh, in_specs=in_specs, out_specs=out_specs, check_vma=False)
```

```python
import functools
import math

import jax
import jax.numpy as jnp
from jax import lax
from jax.experimental import pallas as pl
from jax.experimental.pallas import tpu as pltpu
from jax.sharding import PartitionSpec as P

MESH = pl.DeviceIdType.MESH
F32 = jnp.float32
BF16 = jnp.bfloat16
HEAD = 128
ITERS = 5
TOK = 128
D = 5120
COLS = 2048
HALF = 1024
PAIR = 256
ROWS = 320
OWN = 160
CH = 256
NCH = D // CH
FAR = (2, 1, 3)
ORDER = (2, 1, 3, 0)
PLAN = (
    ((0, 0, 0, 2), (0, 0, 0, 2)),
    ((5, 5, 4, 8), (0, 0, 1, 8)),
    ((20, 20, 20, 20), (6, 8, 11, 20)),
    ((20, 20, 20, 20), (8, 10, 13, 20)),
    ((20, 20, 20, 20), (11, 14, 17, 20)),
    ((20, 20, 20, 20), (13, 16, 19, 20)),
    ((20, 20, 20, 20), (17, 19, 20, 20)),
    ((20, 20, 20, 20), (20, 20, 20, 20)),
)

momentum_rate = 0.95
quintic_a = 3.4445
quintic_b = -4.775
quintic_c = 2.0315
epsilon = 1e-07


def mod4(v):
    return lax.rem(v, 4)


def split(a):
    high = a.astype(BF16)
    rest = a - high.astype(F32)
    mid = rest.astype(BF16)
    return high, mid, (rest - mid.astype(F32)).astype(BF16)


def mm(sa, sb):
    a1, a2, a3 = sa
    b1, b2, b3 = sb
    right = jnp.concatenate([jnp.concatenate([b2, b3], 1), jnp.concatenate([b1, b2], 1)], 0)
    small = jnp.dot(jnp.concatenate([a1, a2], 1), right, preferred_element_type=F32)
    big = jnp.dot(jnp.concatenate([a1, a3], 1), jnp.concatenate([b1, b1], 0), preferred_element_type=F32)
    return big + (small[:, :HEAD] + small[:, HEAD:])


def newton_schulz(gram, scale):
    rows = lax.broadcasted_iota(jnp.int32, (HEAD, HEAD), 0)
    cols = lax.broadcasted_iota(jnp.int32, (HEAD, HEAD), 1)
    eye = (rows == cols).astype(F32)
    trace = jnp.sum(jnp.sum(gram * eye, axis=1, keepdims=True), axis=0, keepdims=True)
    inv = 1.0 / (jnp.sqrt(trace) + epsilon)
    a = (gram * inv) * inv
    q = None
    for step in range(ITERS):
        sa = split(a)
        m = quintic_a * eye + quintic_b * a + quintic_c * mm(sa, sa)
        sm = split(m)
        q = m if q is None else mm(split(q), sm)
        if step < ITERS - 1:
            a = mm(split(mm(sm, sa)), sm)
    return q * (inv * scale)


def kernel(
    acts_h, cot_h, kv_h, w_h, mom_h, upd_o, ig_o,
    acts_v, acts_t, acts_g, kv_v, kv_g, w_v, part, trans, acc, rbuf, mom_v, buf,
    tot, upd, gin, gout, own_v,
    ld_sem, w_sem, send_sem, kv_recv, kvf_recv, ac_recv, tr_recv, rs_recv,
    mom_recv, ch_send, ch_recv, ig_sem, t_recv, o_recv,
):
    z = lax.axis_index("pipe")
    d = lax.axis_index("dp")
    y, x, c = lax.div(d, 8), mod4(lax.div(d, 2)), lax.rem(d, 2)
    e = 1 - c
    pg = x * e + y * c
    pr = y * e + x * c

    def chip(yy, xx, cc):
        return (z, (mod4(yy) * 4 + mod4(xx)) * 2 + cc)

    def on_g(o):
        return chip(y + o * c, x + o * e, c)

    def on_r(o):
        return chip(y + o * e, x + o * c, c)

    sib = chip(y, x, e)
    bar = pltpu.get_barrier_semaphore()

    def greet(dev):
        pl.semaphore_signal(bar, inc=1, device_id=dev, device_id_type=MESH)

    for o in FAR:
        greet(on_g(o))
        greet(chip(y + o * c, x + o * e, e))
        greet(on_r(o))
    greet(sib)

    @pl.when(z < 3)
    def _():
        greet((z + 1, d))

    def start(cp):
        cp.start()
        return cp

    def remote(src, dst, ssem, rsem, dev):
        return pltpu.make_async_remote_copy(src, dst, ssem, rsem, device_id=dev, device_id_type=MESH)

    sends = []

    def send(src, dst, rsem, dev):
        sends.append(start(remote(src, dst, send_sem.at[len(sends)], rsem, dev)))

    def wait(ref, sem):
        pltpu.make_async_copy(ref, ref, sem).wait()

    def cols(k):
        return pl.ds(pl.multiple_of(k * CH, CH), CH)

    ld_kv = start(pltpu.make_async_copy(kv_h, kv_v, ld_sem.at[0]))
    ld_acts = start(pltpu.make_async_copy(acts_h, acts_v, ld_sem.at[1]))
    myrow = pl.multiple_of(c * OWN, OWN)
    sibrow = pl.multiple_of(e * OWN, OWN)
    mycol = pl.multiple_of(c * HALF, HALF)
    sibcol = pl.multiple_of(e * HALF, HALF)
    ld_mom = start(pltpu.make_async_copy(mom_h.at[:, pl.ds(mycol, HALF)], mom_v.at[pl.ds(myrow, OWN)], ld_sem.at[2]))

    @pl.loop(0, NCH)
    def _(k):
        pltpu.make_async_copy(w_h.at[pl.ds(pl.multiple_of(k * CH, CH), CH)], w_v.at[k], w_sem.at[k]).start()

    @pl.when(z == 3)
    def _():
        @pl.loop(0, NCH)
        def _(k):
            pltpu.make_async_copy(cot_h.at[:, cols(k)], gin.at[k], ch_recv.at[k]).start()

    pl.semaphore_wait(bar, jnp.where(z > 0, 11, 10))

    def toks(slot, first=0, count=TOK):
        return pl.ds(pl.multiple_of(slot * TOK + first, count), count)

    slots = (x * 2 + c, y * 2 + c)
    slot_own = pg * 2 + c
    slot_sib = pr * 2 + c

    def near(off, cc):
        return mod4(pg + 4 - off) * 2 + cc

    def send_kv(o):
        at = (mod4(y + o) * PAIR, mod4(x + o) * PAIR + HALF)
        for off in (1, 3):
            for t in (0, 1):
                dev = chip(y, x + off, 0) if t == 0 else chip(y + off, x, 1)
                send(kv_v.at[:, pl.ds(pl.multiple_of(at[t], PAIR), PAIR)],
                     kv_g.at[o, toks(slots[t])], kv_recv.at[o, off, c], dev)
        own_at = pl.multiple_of(mod4(pr + o) * PAIR + mycol, PAIR)
        sib_at = pl.multiple_of(mod4(pg + o) * PAIR + sibcol, PAIR)
        start(pltpu.make_async_copy(kv_v.at[:, pl.ds(own_at, PAIR)], kv_g.at[o, toks(slot_own)], kv_recv.at[o, 0, c]))
        send(kv_v.at[:, pl.ds(sib_at, PAIR)], kv_g.at[o, toks(slot_sib)], kv_recv.at[o, 0, c], sib)

    def pass_kv(o):
        for off in (1, 3, 0):
            for cc in (0, 1):
                wait(kv_g.at[o, toks(near(off, cc))], kv_recv.at[o, off, cc])
                if off:
                    piece = kv_g.at[o, toks(near(off, cc), 0 if off == 1 else 64, 64)]
                    send(piece, piece, kvf_recv.at[o, off // 2, cc], on_g(off))

    def wait_far(o):
        for half in range(2):
            for cc in (0, 1):
                wait(kv_g.at[o, toks(near(2, cc), half * 64, 64)], kvf_recv.at[o, half, cc])

    ld_kv.wait()
    for o in FAR:
        send_kv(o)

    def product(k):
        wait(w_v.at[k], w_sem.at[k])
        own_v[k] = lax.dot_general(kv_v[...], w_v[k], (((1,), (1,)), ((), ())), preferred_element_type=F32)

    def relay(k):
        wait(gin.at[k], ch_recv.at[k])
        gout[k] = (gin[k].astype(F32) + own_v[k]).astype(BF16)

        @pl.when(z > 0)
        def _():
            remote(gout.at[k], gin.at[k], ch_send.at[k], ch_recv.at[k], (z - 1, d)).start()

        pltpu.make_async_copy(gout.at[k], ig_o.at[:, cols(k)], ig_sem.at[k]).start()

    done = [0, 0]

    def chain(ahead, upto):
        ready, sent = (jnp.where(z == 0, a[0], jnp.where(z == 1, a[1], jnp.where(z == 2, a[2], a[3]))) for a in (ahead, upto))

        @pl.loop(0, jnp.maximum(ready - done[0], sent - done[1]))
        def _(n):
            @pl.when(done[0] + n < ready)
            def _():
                product(done[0] + n)

            @pl.when(done[1] + n < sent)
            def _():
                relay(done[1] + n)

        done[:] = [ready, sent]

    chain(*PLAN[0])

    send(mom_h.at[:, pl.ds(sibcol, HALF)], mom_v.at[pl.ds(myrow, OWN)], mom_recv.at[0], sib)
    ld_acts.wait()

    @pl.loop(0, D // 512)
    def _(k):
        at = pl.multiple_of(k * 512, 512)
        acts_t[pl.ds(at, 512), :] = acts_v[:, pl.ds(at, 512)].T

    def send_acts(b):
        rows = pl.ds(b * ROWS, ROWS)

        def source(block):
            return acts_t.at[pl.ds(pl.multiple_of(block * ROWS, ROWS), ROWS)]

        for off in FAR:
            for t in (0, 1):
                block, dev = (b * 4 + mod4(x + off), chip(y, x + off, 0)) if t == 0 else (mod4(y + off) * 4 + b, chip(y + off, x, 1))
                send(source(block), acts_g.at[rows, toks(slots[t])], ac_recv.at[b, off, c], dev)
        start(pltpu.make_async_copy(
            source((b * 4 + x) * e + (y * 4 + b) * c), acts_g.at[rows, toks(slot_own)], ac_recv.at[b, 0, c]))
        send(source((b * 4 + x) * c + (y * 4 + b) * e), acts_g.at[rows, toks(slot_sib)], ac_recv.at[b, 0, c], sib)

    def half_rows(half):
        return pl.ds(half * 2 * ROWS, 2 * ROWS)

    def block(o):
        at = pl.ds(pl.multiple_of(mod4(pr + o) * PAIR, PAIR), PAIR)
        mom = mom_v[:, at].astype(F32) * momentum_rate
        for b in range(4):
            rows = pl.ds(b * ROWS, ROWS)
            term = jnp.dot(acts_g[rows, :], kv_g[o], preferred_element_type=F32)
            term = term + mom * jnp.where(pr == b, 4096.0, 0.0)
            if o == 2:
                part[1, 0, rows, :] = term[:, :HEAD].astype(BF16)
                part[1, 1, rows, :] = term[:, HEAD:].astype(BF16)
            else:
                acc[o, rows, :] = term

    send_acts(0)
    chain(*PLAN[1])
    for o in FAR:
        pass_kv(o)
    for b in (1, 2, 3):
        send_acts(b)
    send_kv(0)
    chain(*PLAN[2])
    for o in FAR:
        wait_far(o)
    ld_mom.wait()
    wait(mom_v.at[pl.ds(sibrow, OWN)], mom_recv.at[0])
    for b in range(4):
        for off in range(4):
            for cc in (0, 1):
                wait(acts_g.at[pl.ds(b * ROWS, ROWS), toks(near(off, cc))], ac_recv.at[b, off, cc])
    block(2)
    for q in range(2):
        for half in range(2):
            send(part.at[1, q, half_rows(half)], trans.at[q, half], tr_recv.at[q, half], on_r(1 + 2 * half))
    pass_kv(0)
    block(1)
    block(3)
    chain(*PLAN[3])
    for q in range(2):
        head = slice(q * HEAD, (q + 1) * HEAD)
        for half in range(2):
            o = 1 + 2 * half
            wait(trans.at[q, half], tr_recv.at[q, half])
            mine, other = half_rows(half), half_rows(1 - half)
            part[o - 1, q, mine, :] = (acc[o, mine, head] + trans[q, half].astype(F32)).astype(BF16)
            part[o - 1, q, other, :] = acc[o, other, head].astype(BF16)
            send(part.at[o - 1, q], rbuf.at[q, half], rs_recv.at[q, half], on_r(o))
    wait_far(0)
    block(0)
    chain(*PLAN[4])

    def gram_of(q):
        head = slice(q * HEAD, (q + 1) * HEAD)
        for half in range(2):
            wait(rbuf.at[q, half], rs_recv.at[q, half])
        total = None
        for b in range(4):
            rows = pl.ds(b * ROWS, ROWS)
            grad = acc[0, rows, head] + rbuf[q, 0, rows, :].astype(F32) + rbuf[q, 1, rows, :].astype(F32)
            value = (grad * (1.0 / 4096)).astype(BF16)
            buf[q, rows, :] = value
            term = lax.dot_general(value, value, (((0,), (0,)), ((), ())), preferred_element_type=F32)
            total = term if total is None else total + term
        tot[q, pg] = total
        for o in FAR:
            send(tot.at[q, pg], tot.at[q, pg], t_recv.at[q, o - 1], on_g(o))

    def iterate(q):
        for o in FAR:
            wait(tot.at[q, mod4(pg + 4 - o)], t_recv.at[q, o - 1])
        scale = 0.2 * math.sqrt(max(D, HEAD))
        high, mid, low = split(newton_schulz((tot[q, 0] + tot[q, 1]) + (tot[q, 2] + tot[q, 3]), scale))
        place = pl.ds(pl.multiple_of(mycol + pr * PAIR + q * HEAD, HEAD), HEAD)
        for o in ORDER:
            first = pl.multiple_of(mod4(pr + o) * ROWS, ROWS)
            value = buf[q, pl.ds(first, ROWS), :]
            total = jnp.dot(value, low, preferred_element_type=F32) + jnp.dot(value, mid, preferred_element_type=F32)
            upd[q, pl.ds(first, ROWS), :] = (total + jnp.dot(value, high, preferred_element_type=F32)).astype(BF16)
            same = upd.at[q, pl.ds(pl.multiple_of(first + myrow, OWN), OWN)]
            cross = upd.at[q, pl.ds(pl.multiple_of(first + sibrow, OWN), OWN)]
            if o:
                send(same, upd_o.at[:, place], o_recv.at[q, 0, o], on_r(o))
                send(cross, upd_o.at[:, place], o_recv.at[q, 1, o], chip(y + o * e, x + o * c, e))
            else:
                start(pltpu.make_async_copy(same, upd_o.at[:, place], o_recv.at[q, 0, 0]))
                send(cross, upd_o.at[:, place], o_recv.at[q, 1, 0], sib)

    gram_of(0)
    chain(*PLAN[5])
    gram_of(1)
    iterate(0)
    chain(*PLAN[6])
    iterate(1)
    chain(*PLAN[7])
    for q in range(2):
        for o in range(4):
            at = pl.multiple_of(mycol + mod4(pr + 4 - o) * PAIR + q * HEAD, HEAD)
            wait(upd_o.at[:, pl.ds(at, HEAD)], o_recv.at[q, 0, o])
            at = pl.multiple_of(sibcol + mod4(pg + 4 - o) * PAIR + q * HEAD, HEAD)
            wait(upd_o.at[:, pl.ds(at, HEAD)], o_recv.at[q, 1, o])
    for cp in sends:
        cp.wait_send()

    @pl.loop(0, NCH)
    def _(k):
        wait(gout.at[k], ig_sem.at[k])

    @pl.when(z > 0)
    def _():
        @pl.loop(0, NCH)
        def _(k):
            remote(gout.at[k], gin.at[k], ch_send.at[k], ch_recv.at[k], (z - 1, d)).wait_send()


def shards(acts, cotangent, kv_grads, w_kv, momentum):
    dma = pltpu.SemaphoreType.DMA
    vmem = pltpu.VMEM
    anyspec = pl.BlockSpec(memory_space=pl.ANY)
    update, grads = pl.pallas_call(
        kernel,
        out_shape=(jax.ShapeDtypeStruct((OWN, COLS), BF16), jax.ShapeDtypeStruct((TOK, D), BF16)),
        in_specs=[anyspec] * 5,
        out_specs=(anyspec, anyspec),
        scratch_shapes=[
            vmem((TOK, D), BF16), vmem((D, TOK), BF16), vmem((4 * ROWS, 8 * TOK), BF16),
            vmem((TOK, COLS), BF16), vmem((4, 8 * TOK, PAIR), BF16), vmem((NCH, CH, COLS), BF16),
            vmem((3, 2, 4 * ROWS, HEAD), BF16), vmem((2, 2, 2 * ROWS, HEAD), BF16), vmem((4, 4 * ROWS, PAIR), F32),
            vmem((2, 2, 4 * ROWS, HEAD), BF16), vmem((ROWS, HALF), BF16), vmem((2, 4 * ROWS, HEAD), BF16),
            vmem((2, 4, HEAD, HEAD), F32), vmem((2, 4 * ROWS, HEAD), BF16),
            vmem((NCH, TOK, CH), BF16), vmem((NCH, TOK, CH), BF16), vmem((NCH, TOK, CH), F32),
            dma((3,)), dma((NCH,)), dma((96,)), dma((4, 4, 2)), dma((4, 2, 2)), dma((4, 4, 2)),
            dma((2, 2)), dma((2, 2)), dma((1,)), dma((NCH,)), dma((NCH,)), dma((NCH,)),
            dma((2, 3)), dma((2, 2, 4)),
        ],
        name="muon_back",
        compiler_params=pltpu.CompilerParams(
            collective_id=0, has_side_effects=True, vmem_limit_bytes=60 * 1024 * 1024
        ),
    )(acts[0], cotangent, kv_grads[0], w_kv[0], momentum[0])
    return update[None], grads[None]


def solution(mesh):
    in_specs = (
        P("pipe", "dp", None),
        P("dp", None),
        P("pipe", "dp", None),
        P("pipe", None, None),
        P("pipe", "dp", None),
    )
    out_specs = (P("pipe", "dp", None), P("pipe", "dp", None))
    return jax.shard_map(shards, mesh=mesh, in_specs=in_specs, out_specs=out_specs, check_vma=False)
```

```python
import functools
import math

import jax
import jax.numpy as jnp
from jax import lax
from jax.experimental import pallas as pl
from jax.experimental.pallas import tpu as pltpu
from jax.sharding import PartitionSpec as P

MESH = pl.DeviceIdType.MESH
F32 = jnp.float32
BF16 = jnp.bfloat16
HEAD = 128
ITERS = 5
TOK = 128
D = 5120
COLS = 2048
HALF = 1024
PAIR = 256
ROWS = 320
OWN = 160
CH = 256
NCH = D // CH
FAR = (2, 1, 3)
ORDER = (2, 1, 3, 0)
PLAN = (
    ((0, 0, 0, 2), (0, 0, 0, 2)),
    ((5, 5, 4, 6), (0, 0, 1, 5)),
    ((13, 13, 12, 14), (0, 2, 6, 9)),
    ((13, 13, 12, 14), (0, 2, 6, 9)),
    ((17, 17, 16, 18), (0, 4, 8, 12)),
    ((20, 20, 20, 20), (2, 6, 10, 14)),
    ((20, 20, 20, 20), (4, 8, 13, 17)),
    ((20, 20, 20, 20), (5, 10, 15, 19)),
    ((20, 20, 20, 20), (8, 13, 18, 20)),
    ((20, 20, 20, 20), (10, 15, 20, 20)),
    ((20, 20, 20, 20), (13, 18, 20, 20)),
    ((20, 20, 20, 20), (13, 19, 20, 20)),
    ((20, 20, 20, 20), (20, 20, 20, 20)),
)

momentum_rate = 0.95
quintic_a = 3.4445
quintic_b = -4.775
quintic_c = 2.0315
epsilon = 1e-07


def mod4(v):
    return lax.rem(v, 4)


def split(a):
    high = a.astype(BF16)
    rest = a - high.astype(F32)
    mid = rest.astype(BF16)
    return high, mid, (rest - mid.astype(F32)).astype(BF16)


def mm(sa, sb):
    a1, a2, a3 = sa
    b1, b2, b3 = sb
    right = jnp.concatenate([jnp.concatenate([b2, b3], 1), jnp.concatenate([b1, b2], 1)], 0)
    small = jnp.dot(jnp.concatenate([a1, a2], 1), right, preferred_element_type=F32)
    big = jnp.dot(jnp.concatenate([a1, a3], 1), jnp.concatenate([b1, b1], 0), preferred_element_type=F32)
    return big + (small[:, :HEAD] + small[:, HEAD:])


def newton_schulz(gram, scale):
    rows = lax.broadcasted_iota(jnp.int32, (HEAD, HEAD), 0)
    cols = lax.broadcasted_iota(jnp.int32, (HEAD, HEAD), 1)
    eye = (rows == cols).astype(F32)
    trace = jnp.sum(jnp.sum(gram * eye, axis=1, keepdims=True), axis=0, keepdims=True)
    inv = 1.0 / (jnp.sqrt(trace) + epsilon)
    a = (gram * inv) * inv
    q = None
    for step in range(ITERS):
        sa = split(a)
        m = quintic_a * eye + quintic_b * a + quintic_c * mm(sa, sa)
        sm = split(m)
        q = m if q is None else mm(split(q), sm)
        if step < ITERS - 1:
            a = mm(split(mm(sm, sa)), sm)
    return q * (inv * scale)


def kernel(
    acts_h, cot_h, kv_h, w_h, mom_h, upd_o, ig_o,
    acts_v, acts_t, acts_g, kv_v, kv_g, w_v, part, trans, acc, rbuf, mom_v, buf,
    tot, upd, gin, gout, own_v,
    ld_sem, w_sem, send_sem, kv_recv, kvf_recv, ac_recv, tr_recv, rs_recv,
    mom_recv, ch_send, ch_recv, ig_sem, t_recv, o_recv,
):
    z = lax.axis_index("pipe")
    d = lax.axis_index("dp")
    y, x, c = lax.div(d, 8), mod4(lax.div(d, 2)), lax.rem(d, 2)
    e = 1 - c
    pg = x * e + y * c
    pr = y * e + x * c

    def chip(yy, xx, cc):
        return (z, (mod4(yy) * 4 + mod4(xx)) * 2 + cc)

    def on_g(o):
        return chip(y + o * c, x + o * e, c)

    def on_r(o):
        return chip(y + o * e, x + o * c, c)

    sib = chip(y, x, e)
    bar = pltpu.get_barrier_semaphore()

    def greet(dev):
        pl.semaphore_signal(bar, inc=1, device_id=dev, device_id_type=MESH)

    for o in FAR:
        greet(on_g(o))
        greet(chip(y + o * c, x + o * e, e))
        greet(on_r(o))
    greet(sib)

    @pl.when(z < 3)
    def _():
        greet((z + 1, d))

    def start(cp):
        cp.start()
        return cp

    def remote(src, dst, ssem, rsem, dev):
        return pltpu.make_async_remote_copy(src, dst, ssem, rsem, device_id=dev, device_id_type=MESH)

    sends = []

    def send(src, dst, rsem, dev):
        sends.append(start(remote(src, dst, send_sem.at[len(sends)], rsem, dev)))

    def wait(ref, sem):
        pltpu.make_async_copy(ref, ref, sem).wait()

    def cols(k):
        return pl.ds(pl.multiple_of(k * CH, CH), CH)

    ld_kv = start(pltpu.make_async_copy(kv_h, kv_v, ld_sem.at[0]))
    ld_acts = start(pltpu.make_async_copy(acts_h, acts_v, ld_sem.at[1]))
    myrow = pl.multiple_of(c * OWN, OWN)
    sibrow = pl.multiple_of(e * OWN, OWN)
    mycol = pl.multiple_of(c * HALF, HALF)
    sibcol = pl.multiple_of(e * HALF, HALF)
    ld_mom = start(pltpu.make_async_copy(mom_h.at[:, pl.ds(mycol, HALF)], mom_v.at[pl.ds(myrow, OWN)], ld_sem.at[2]))

    @pl.loop(0, NCH)
    def _(k):
        pltpu.make_async_copy(w_h.at[pl.ds(pl.multiple_of(k * CH, CH), CH)], w_v.at[k], w_sem.at[k]).start()

    @pl.when(z == 3)
    def _():
        @pl.loop(0, NCH)
        def _(k):
            pltpu.make_async_copy(cot_h.at[:, cols(k)], gin.at[k], ch_recv.at[k]).start()

    pl.semaphore_wait(bar, jnp.where(z > 0, 11, 10))

    def toks(slot, first=0, count=TOK):
        return pl.ds(pl.multiple_of(slot * TOK + first, count), count)

    slots = (x * 2 + c, y * 2 + c)
    slot_own = pg * 2 + c
    slot_sib = pr * 2 + c

    def near(off, cc):
        return mod4(pg + 4 - off) * 2 + cc

    def send_kv(o):
        at = (mod4(y + o) * PAIR, mod4(x + o) * PAIR + HALF)
        for off in (1, 3):
            for t in (0, 1):
                dev = chip(y, x + off, 0) if t == 0 else chip(y + off, x, 1)
                send(kv_v.at[:, pl.ds(pl.multiple_of(at[t], PAIR), PAIR)],
                     kv_g.at[o, toks(slots[t])], kv_recv.at[o, off, c], dev)
        own_at = pl.multiple_of(mod4(pr + o) * PAIR + mycol, PAIR)
        sib_at = pl.multiple_of(mod4(pg + o) * PAIR + sibcol, PAIR)
        start(pltpu.make_async_copy(kv_v.at[:, pl.ds(own_at, PAIR)], kv_g.at[o, toks(slot_own)], kv_recv.at[o, 0, c]))
        send(kv_v.at[:, pl.ds(sib_at, PAIR)], kv_g.at[o, toks(slot_sib)], kv_recv.at[o, 0, c], sib)

    def pass_kv(o):
        for off in (1, 3, 0):
            for cc in (0, 1):
                wait(kv_g.at[o, toks(near(off, cc))], kv_recv.at[o, off, cc])
                if off:
                    piece = kv_g.at[o, toks(near(off, cc), 0 if off == 1 else 64, 64)]
                    send(piece, piece, kvf_recv.at[o, off // 2, cc], on_g(off))

    def wait_far(o):
        for half in range(2):
            for cc in (0, 1):
                wait(kv_g.at[o, toks(near(2, cc), half * 64, 64)], kvf_recv.at[o, half, cc])

    ld_kv.wait()
    for o in FAR:
        send_kv(o)

    def product(k):
        wait(w_v.at[k], w_sem.at[k])
        own_v[k] = lax.dot_general(kv_v[...], w_v[k], (((1,), (1,)), ((), ())), preferred_element_type=F32)

    def relay(k):
        wait(gin.at[k], ch_recv.at[k])
        gout[k] = (gin[k].astype(F32) + own_v[k]).astype(BF16)

        @pl.when(z > 0)
        def _():
            remote(gout.at[k], gin.at[k], ch_send.at[k], ch_recv.at[k], (z - 1, d)).start()

        pltpu.make_async_copy(gout.at[k], ig_o.at[:, cols(k)], ig_sem.at[k]).start()

    done = [0, 0]

    def chain(ahead, upto):
        ready, sent = (jnp.where(z == 0, a[0], jnp.where(z == 1, a[1], jnp.where(z == 2, a[2], a[3]))) for a in (ahead, upto))

        @pl.loop(0, jnp.maximum(ready - done[0], sent - done[1]))
        def _(n):
            @pl.when(done[0] + n < ready)
            def _():
                product(done[0] + n)

            @pl.when(done[1] + n < sent)
            def _():
                relay(done[1] + n)

        done[:] = [ready, sent]

    chain(*PLAN[0])

    send(mom_h.at[:, pl.ds(sibcol, HALF)], mom_v.at[pl.ds(myrow, OWN)], mom_recv.at[0], sib)
    ld_acts.wait()

    @pl.loop(0, D // 512)
    def _(k):
        at = pl.multiple_of(k * 512, 512)
        acts_t[pl.ds(at, 512), :] = acts_v[:, pl.ds(at, 512)].T

    def send_acts(b):
        rows = pl.ds(b * ROWS, ROWS)

        def source(block):
            return acts_t.at[pl.ds(pl.multiple_of(block * ROWS, ROWS), ROWS)]

        for off in FAR:
            for t in (0, 1):
                block, dev = (b * 4 + mod4(x + off), chip(y, x + off, 0)) if t == 0 else (mod4(y + off) * 4 + b, chip(y + off, x, 1))
                send(source(block), acts_g.at[rows, toks(slots[t])], ac_recv.at[b, off, c], dev)
        start(pltpu.make_async_copy(
            source((b * 4 + x) * e + (y * 4 + b) * c), acts_g.at[rows, toks(slot_own)], ac_recv.at[b, 0, c]))
        send(source((b * 4 + x) * c + (y * 4 + b) * e), acts_g.at[rows, toks(slot_sib)], ac_recv.at[b, 0, c], sib)

    def half_rows(half):
        return pl.ds(half * 2 * ROWS, 2 * ROWS)

    def block(o, b):
        at = pl.ds(pl.multiple_of(mod4(pr + o) * PAIR, PAIR), PAIR)
        rows = pl.ds(b * ROWS, ROWS)
        term = jnp.dot(acts_g[rows, :], kv_g[o], preferred_element_type=F32)
        term = term + (mom_v[:, at].astype(F32) * momentum_rate) * jnp.where(pr == b, 4096.0, 0.0)
        if o == 2:
            part[1, 0, rows, :] = term[:, :HEAD].astype(BF16)
            part[1, 1, rows, :] = term[:, HEAD:].astype(BF16)
        else:
            acc[o, rows, :] = term

    send_acts(0)
    chain(*PLAN[1])
    for o in FAR:
        pass_kv(o)
    for b in (1, 2, 3):
        send_acts(b)
    send_kv(0)
    chain(*PLAN[2])
    for o in FAR:
        wait_far(o)
    ld_mom.wait()
    wait(mom_v.at[pl.ds(sibrow, OWN)], mom_recv.at[0])
    for b in range(4):
        chain(*PLAN[3 + b])
        for off in range(4):
            for cc in (0, 1):
                wait(acts_g.at[pl.ds(b * ROWS, ROWS), toks(near(off, cc))], ac_recv.at[b, off, cc])
        block(2, b)
        if b % 2:
            half = b // 2
            for q in range(2):
                send(part.at[1, q, half_rows(half)], trans.at[q, half], tr_recv.at[q, half], on_r(1 + 2 * half))
        block(1, b)
        block(3, b)
    pass_kv(0)
    chain(*PLAN[7])
    for q in range(2):
        head = slice(q * HEAD, (q + 1) * HEAD)
        for half in range(2):
            o = 1 + 2 * half
            wait(trans.at[q, half], tr_recv.at[q, half])
            mine, other = half_rows(half), half_rows(1 - half)
            part[o - 1, q, mine, :] = (acc[o, mine, head] + trans[q, half].astype(F32)).astype(BF16)
            part[o - 1, q, other, :] = acc[o, other, head].astype(BF16)
            send(part.at[o - 1, q], rbuf.at[q, half], rs_recv.at[q, half], on_r(o))
    wait_far(0)
    for b in range(4):
        block(0, b)
    chain(*PLAN[8])

    def gram_of(q):
        head = slice(q * HEAD, (q + 1) * HEAD)
        for half in range(2):
            wait(rbuf.at[q, half], rs_recv.at[q, half])
        total = None
        for b in range(4):
            rows = pl.ds(b * ROWS, ROWS)
            grad = acc[0, rows, head] + rbuf[q, 0, rows, :].astype(F32) + rbuf[q, 1, rows, :].astype(F32)
            value = (grad * (1.0 / 4096)).astype(BF16)
            buf[q, rows, :] = value
            term = lax.dot_general(value, value, (((0,), (0,)), ((), ())), preferred_element_type=F32)
            total = term if total is None else total + term
        tot[q, pg] = total
        for o in FAR:
            send(tot.at[q, pg], tot.at[q, pg], t_recv.at[q, o - 1], on_g(o))

    def iterate(q):
        for o in FAR:
            wait(tot.at[q, mod4(pg + 4 - o)], t_recv.at[q, o - 1])
        scale = 0.2 * math.sqrt(max(D, HEAD))
        high, mid, low = split(newton_schulz((tot[q, 0] + tot[q, 1]) + (tot[q, 2] + tot[q, 3]), scale))
        place = pl.ds(pl.multiple_of(mycol + pr * PAIR + q * HEAD, HEAD), HEAD)
        for o in ORDER:
            first = pl.multiple_of(mod4(pr + o) * ROWS, ROWS)
            value = buf[q, pl.ds(first, ROWS), :]
            total = jnp.dot(value, low, preferred_element_type=F32) + jnp.dot(value, mid, preferred_element_type=F32)
            upd[q, pl.ds(first, ROWS), :] = (total + jnp.dot(value, high, preferred_element_type=F32)).astype(BF16)
            same = upd.at[q, pl.ds(pl.multiple_of(first + myrow, OWN), OWN)]
            cross = upd.at[q, pl.ds(pl.multiple_of(first + sibrow, OWN), OWN)]
            if o:
                send(same, upd_o.at[:, place], o_recv.at[q, 0, o], on_r(o))
                send(cross, upd_o.at[:, place], o_recv.at[q, 1, o], chip(y + o * e, x + o * c, e))
            else:
                start(pltpu.make_async_copy(same, upd_o.at[:, place], o_recv.at[q, 0, 0]))
                send(cross, upd_o.at[:, place], o_recv.at[q, 1, 0], sib)

    gram_of(0)
    chain(*PLAN[9])
    gram_of(1)
    iterate(0)
    chain(*PLAN[10])
    iterate(1)
    chain(*PLAN[12])
    for q in range(2):
        for o in range(4):
            at = pl.multiple_of(mycol + mod4(pr + 4 - o) * PAIR + q * HEAD, HEAD)
            wait(upd_o.at[:, pl.ds(at, HEAD)], o_recv.at[q, 0, o])
            at = pl.multiple_of(sibcol + mod4(pg + 4 - o) * PAIR + q * HEAD, HEAD)
            wait(upd_o.at[:, pl.ds(at, HEAD)], o_recv.at[q, 1, o])
    for cp in sends:
        cp.wait_send()

    @pl.loop(0, NCH)
    def _(k):
        wait(gout.at[k], ig_sem.at[k])

    @pl.when(z > 0)
    def _():
        @pl.loop(0, NCH)
        def _(k):
            remote(gout.at[k], gin.at[k], ch_send.at[k], ch_recv.at[k], (z - 1, d)).wait_send()


def shards(acts, cotangent, kv_grads, w_kv, momentum):
    dma = pltpu.SemaphoreType.DMA
    vmem = pltpu.VMEM
    anyspec = pl.BlockSpec(memory_space=pl.ANY)
    update, grads = pl.pallas_call(
        kernel,
        out_shape=(jax.ShapeDtypeStruct((OWN, COLS), BF16), jax.ShapeDtypeStruct((TOK, D), BF16)),
        in_specs=[anyspec] * 5,
        out_specs=(anyspec, anyspec),
        scratch_shapes=[
            vmem((TOK, D), BF16), vmem((D, TOK), BF16), vmem((4 * ROWS, 8 * TOK), BF16),
            vmem((TOK, COLS), BF16), vmem((4, 8 * TOK, PAIR), BF16), vmem((NCH, CH, COLS), BF16),
            vmem((3, 2, 4 * ROWS, HEAD), BF16), vmem((2, 2, 2 * ROWS, HEAD), BF16), vmem((4, 4 * ROWS, PAIR), F32),
            vmem((2, 2, 4 * ROWS, HEAD), BF16), vmem((ROWS, HALF), BF16), vmem((2, 4 * ROWS, HEAD), BF16),
            vmem((2, 4, HEAD, HEAD), F32), vmem((2, 4 * ROWS, HEAD), BF16),
            vmem((NCH, TOK, CH), BF16), vmem((NCH, TOK, CH), BF16), vmem((NCH, TOK, CH), F32),
            dma((3,)), dma((NCH,)), dma((96,)), dma((4, 4, 2)), dma((4, 2, 2)), dma((4, 4, 2)),
            dma((2, 2)), dma((2, 2)), dma((1,)), dma((NCH,)), dma((NCH,)), dma((NCH,)),
            dma((2, 3)), dma((2, 2, 4)),
        ],
        name="muon_back",
        compiler_params=pltpu.CompilerParams(
            collective_id=0, has_side_effects=True, vmem_limit_bytes=60 * 1024 * 1024
        ),
    )(acts[0], cotangent, kv_grads[0], w_kv[0], momentum[0])
    return update[None], grads[None]


def solution(mesh):
    in_specs = (
        P("pipe", "dp", None),
        P("dp", None),
        P("pipe", "dp", None),
        P("pipe", None, None),
        P("pipe", "dp", None),
    )
    out_specs = (P("pipe", "dp", None), P("pipe", "dp", None))
    return jax.shard_map(shards, mesh=mesh, in_specs=in_specs, out_specs=out_specs, check_vma=False)
```

```python
import functools
import math

import jax
import jax.numpy as jnp
from jax import lax
from jax.experimental import pallas as pl
from jax.experimental.pallas import tpu as pltpu
from jax.sharding import PartitionSpec as P

MESH = pl.DeviceIdType.MESH
F32 = jnp.float32
BF16 = jnp.bfloat16
HEAD = 128
ITERS = 5
TOK = 128
D = 5120
COLS = 2048
HALF = 1024
PAIR = 256
ROWS = 320
OWN = 160
CH = 256
NCH = D // CH
FAR = (2, 1, 3)
ORDER = (2, 1, 3, 0)
PLAN = (
    ((0, 0, 0, 2), (0, 0, 0, 2)),
    ((5, 5, 4, 6), (0, 0, 1, 5)),
    ((13, 13, 12, 14), (0, 2, 6, 9)),
    ((13, 13, 12, 14), (0, 2, 6, 9)),
    ((17, 17, 16, 18), (0, 4, 8, 12)),
    ((20, 20, 20, 20), (2, 6, 10, 14)),
    ((20, 20, 20, 20), (4, 8, 13, 17)),
    ((20, 20, 20, 20), (5, 10, 15, 19)),
    ((20, 20, 20, 20), (8, 13, 18, 20)),
    ((20, 20, 20, 20), (10, 15, 20, 20)),
    ((20, 20, 20, 20), (13, 18, 20, 20)),
    ((20, 20, 20, 20), (13, 19, 20, 20)),
    ((20, 20, 20, 20), (20, 20, 20, 20)),
)

momentum_rate = 0.95
quintic_a = 3.4445
quintic_b = -4.775
quintic_c = 2.0315
epsilon = 1e-07


def mod4(v):
    return lax.rem(v, 4)


def split(a):
    high = a.astype(BF16)
    rest = a - high.astype(F32)
    mid = rest.astype(BF16)
    return high, mid, (rest - mid.astype(F32)).astype(BF16)


def mm(sa, sb):
    a1, a2, a3 = sa
    b1, b2, b3 = sb
    right = jnp.concatenate([jnp.concatenate([b2, b3], 1), jnp.concatenate([b1, b2], 1)], 0)
    small = jnp.dot(jnp.concatenate([a1, a2], 1), right, preferred_element_type=F32)
    big = jnp.dot(jnp.concatenate([a1, a3], 1), jnp.concatenate([b1, b1], 0), preferred_element_type=F32)
    return big + (small[:, :HEAD] + small[:, HEAD:])


def newton_schulz(gram, scale):
    rows = lax.broadcasted_iota(jnp.int32, (HEAD, HEAD), 0)
    cols = lax.broadcasted_iota(jnp.int32, (HEAD, HEAD), 1)
    eye = (rows == cols).astype(F32)
    trace = jnp.sum(jnp.sum(gram * eye, axis=1, keepdims=True), axis=0, keepdims=True)
    inv = 1.0 / (jnp.sqrt(trace) + epsilon)
    a = (gram * inv) * inv
    q = None
    for step in range(ITERS):
        sa = split(a)
        m = quintic_a * eye + quintic_b * a + quintic_c * mm(sa, sa)
        sm = split(m)
        q = m if q is None else mm(split(q), sm)
        if step < ITERS - 1:
            a = mm(split(mm(sm, sa)), sm)
    return q * (inv * scale)


def kernel(
    acts_h, cot_h, kv_h, w_h, mom_h, upd_o, gout,
    acts_v, acts_t, acts_g, kv_v, kv_g, w_v, part, trans, acc, rbuf, mom_v, buf,
    tot, upd, gin, own_v,
    ld_sem, w_sem, send_sem, kv_recv, kvf_recv, ac_recv, tr_recv, rs_recv,
    mom_recv, ch_send, ch_recv, t_recv, o_recv,
):
    z = lax.axis_index("pipe")
    d = lax.axis_index("dp")
    y, x, c = lax.div(d, 8), mod4(lax.div(d, 2)), lax.rem(d, 2)
    e = 1 - c
    pg = x * e + y * c
    pr = y * e + x * c

    def chip(yy, xx, cc):
        return (z, (mod4(yy) * 4 + mod4(xx)) * 2 + cc)

    def on_g(o):
        return chip(y + o * c, x + o * e, c)

    def on_r(o):
        return chip(y + o * e, x + o * c, c)

    sib = chip(y, x, e)
    bar = pltpu.get_barrier_semaphore()

    def greet(dev):
        pl.semaphore_signal(bar, inc=1, device_id=dev, device_id_type=MESH)

    for o in FAR:
        greet(on_g(o))
        greet(chip(y + o * c, x + o * e, e))
        greet(on_r(o))
    greet(sib)

    @pl.when(z < 3)
    def _():
        greet((z + 1, d))

    def start(cp):
        cp.start()
        return cp

    def remote(src, dst, ssem, rsem, dev):
        return pltpu.make_async_remote_copy(src, dst, ssem, rsem, device_id=dev, device_id_type=MESH)

    sends = []

    def send(src, dst, rsem, dev):
        sends.append(start(remote(src, dst, send_sem.at[len(sends)], rsem, dev)))

    def wait(ref, sem):
        pltpu.make_async_copy(ref, ref, sem).wait()

    def cols(k):
        return pl.ds(pl.multiple_of(k * CH, CH), CH)

    ld_kv = start(pltpu.make_async_copy(kv_h, kv_v, ld_sem.at[0]))
    ld_acts = start(pltpu.make_async_copy(acts_h, acts_v, ld_sem.at[1]))
    myrow = pl.multiple_of(c * OWN, OWN)
    sibrow = pl.multiple_of(e * OWN, OWN)
    mycol = pl.multiple_of(c * HALF, HALF)
    sibcol = pl.multiple_of(e * HALF, HALF)
    ld_mom = start(pltpu.make_async_copy(mom_h.at[:, pl.ds(mycol, HALF)], mom_v.at[pl.ds(myrow, OWN)], ld_sem.at[2]))

    @pl.loop(0, NCH)
    def _(k):
        pltpu.make_async_copy(w_h.at[pl.ds(pl.multiple_of(k * CH, CH), CH)], w_v.at[k], w_sem.at[k]).start()

    @pl.when(z == 3)
    def _():
        @pl.loop(0, NCH)
        def _(k):
            pltpu.make_async_copy(cot_h.at[:, cols(k)], gin.at[k], ch_recv.at[k]).start()

    pl.semaphore_wait(bar, jnp.where(z > 0, 11, 10))

    def toks(slot, first=0, count=TOK):
        return pl.ds(pl.multiple_of(slot * TOK + first, count), count)

    slots = (x * 2 + c, y * 2 + c)
    slot_own = pg * 2 + c
    slot_sib = pr * 2 + c

    def near(off, cc):
        return mod4(pg + 4 - off) * 2 + cc

    def send_kv(o):
        at = (mod4(y + o) * PAIR, mod4(x + o) * PAIR + HALF)
        for off in (1, 3):
            for t in (0, 1):
                dev = chip(y, x + off, 0) if t == 0 else chip(y + off, x, 1)
                send(kv_v.at[:, pl.ds(pl.multiple_of(at[t], PAIR), PAIR)],
                     kv_g.at[o, toks(slots[t])], kv_recv.at[o, off, c], dev)
        own_at = pl.multiple_of(mod4(pr + o) * PAIR + mycol, PAIR)
        sib_at = pl.multiple_of(mod4(pg + o) * PAIR + sibcol, PAIR)
        start(pltpu.make_async_copy(kv_v.at[:, pl.ds(own_at, PAIR)], kv_g.at[o, toks(slot_own)], kv_recv.at[o, 0, c]))
        send(kv_v.at[:, pl.ds(sib_at, PAIR)], kv_g.at[o, toks(slot_sib)], kv_recv.at[o, 0, c], sib)

    def pass_kv(o):
        for off in (1, 3, 0):
            for cc in (0, 1):
                wait(kv_g.at[o, toks(near(off, cc))], kv_recv.at[o, off, cc])
                if off:
                    piece = kv_g.at[o, toks(near(off, cc), 0 if off == 1 else 64, 64)]
                    send(piece, piece, kvf_recv.at[o, off // 2, cc], on_g(off))

    def wait_far(o):
        for half in range(2):
            for cc in (0, 1):
                wait(kv_g.at[o, toks(near(2, cc), half * 64, 64)], kvf_recv.at[o, half, cc])

    ld_kv.wait()
    for o in FAR:
        send_kv(o)

    def product(k):
        wait(w_v.at[k], w_sem.at[k])
        own_v[k] = lax.dot_general(kv_v[...], w_v[k], (((1,), (1,)), ((), ())), preferred_element_type=F32)

    def relay(k):
        wait(gin.at[k], ch_recv.at[k])
        gout[k] = (gin[k].astype(F32) + own_v[k]).astype(BF16)

        @pl.when(z > 0)
        def _():
            remote(gout.at[k], gin.at[k], ch_send.at[k], ch_recv.at[k], (z - 1, d)).start()


    done = [0, 0]

    def chain(ahead, upto):
        ready, sent = (jnp.where(z == 0, a[0], jnp.where(z == 1, a[1], jnp.where(z == 2, a[2], a[3]))) for a in (ahead, upto))

        @pl.loop(0, jnp.maximum(ready - done[0], sent - done[1]))
        def _(n):
            @pl.when(done[0] + n < ready)
            def _():
                product(done[0] + n)

            @pl.when(done[1] + n < sent)
            def _():
                relay(done[1] + n)

        done[:] = [ready, sent]

    chain(*PLAN[0])

    send(mom_h.at[:, pl.ds(sibcol, HALF)], mom_v.at[pl.ds(myrow, OWN)], mom_recv.at[0], sib)
    ld_acts.wait()

    @pl.loop(0, D // 512)
    def _(k):
        at = pl.multiple_of(k * 512, 512)
        acts_t[pl.ds(at, 512), :] = acts_v[:, pl.ds(at, 512)].T

    def send_acts(b):
        rows = pl.ds(b * ROWS, ROWS)

        def source(block):
            return acts_t.at[pl.ds(pl.multiple_of(block * ROWS, ROWS), ROWS)]

        for off in FAR:
            for t in (0, 1):
                block, dev = (b * 4 + mod4(x + off), chip(y, x + off, 0)) if t == 0 else (mod4(y + off) * 4 + b, chip(y + off, x, 1))
                send(source(block), acts_g.at[rows, toks(slots[t])], ac_recv.at[b, off, c], dev)
        start(pltpu.make_async_copy(
            source((b * 4 + x) * e + (y * 4 + b) * c), acts_g.at[rows, toks(slot_own)], ac_recv.at[b, 0, c]))
        send(source((b * 4 + x) * c + (y * 4 + b) * e), acts_g.at[rows, toks(slot_sib)], ac_recv.at[b, 0, c], sib)

    def half_rows(half):
        return pl.ds(half * 2 * ROWS, 2 * ROWS)

    def block(o, b):
        at = pl.ds(pl.multiple_of(mod4(pr + o) * PAIR, PAIR), PAIR)
        rows = pl.ds(b * ROWS, ROWS)
        term = jnp.dot(acts_g[rows, :], kv_g[o], preferred_element_type=F32)
        term = term + (mom_v[:, at].astype(F32) * momentum_rate) * jnp.where(pr == b, 4096.0, 0.0)
        if o == 2:
            part[1, 0, rows, :] = term[:, :HEAD].astype(BF16)
            part[1, 1, rows, :] = term[:, HEAD:].astype(BF16)
        else:
            acc[o, rows, :] = term

    send_acts(0)
    chain(*PLAN[1])
    for o in FAR:
        pass_kv(o)
    for b in (1, 2, 3):
        send_acts(b)
    send_kv(0)
    chain(*PLAN[2])
    for o in FAR:
        wait_far(o)
    ld_mom.wait()
    wait(mom_v.at[pl.ds(sibrow, OWN)], mom_recv.at[0])
    for b in range(4):
        chain(*PLAN[3 + b])
        for off in range(4):
            for cc in (0, 1):
                wait(acts_g.at[pl.ds(b * ROWS, ROWS), toks(near(off, cc))], ac_recv.at[b, off, cc])
        block(2, b)
        if b % 2:
            half = b // 2
            for q in range(2):
                send(part.at[1, q, half_rows(half)], trans.at[q, half], tr_recv.at[q, half], on_r(1 + 2 * half))
        block(1, b)
        block(3, b)
    pass_kv(0)
    chain(*PLAN[7])
    for q in range(2):
        head = slice(q * HEAD, (q + 1) * HEAD)
        for half in range(2):
            o = 1 + 2 * half
            wait(trans.at[q, half], tr_recv.at[q, half])
            mine, other = half_rows(half), half_rows(1 - half)
            part[o - 1, q, mine, :] = (acc[o, mine, head] + trans[q, half].astype(F32)).astype(BF16)
            part[o - 1, q, other, :] = acc[o, other, head].astype(BF16)
            send(part.at[o - 1, q], rbuf.at[q, half], rs_recv.at[q, half], on_r(o))
    wait_far(0)
    for b in range(4):
        block(0, b)
    chain(*PLAN[8])

    def gram_of(q):
        head = slice(q * HEAD, (q + 1) * HEAD)
        for half in range(2):
            wait(rbuf.at[q, half], rs_recv.at[q, half])
        total = None
        for b in range(4):
            rows = pl.ds(b * ROWS, ROWS)
            grad = acc[0, rows, head] + rbuf[q, 0, rows, :].astype(F32) + rbuf[q, 1, rows, :].astype(F32)
            value = (grad * (1.0 / 4096)).astype(BF16)
            buf[q, rows, :] = value
            term = lax.dot_general(value, value, (((0,), (0,)), ((), ())), preferred_element_type=F32)
            total = term if total is None else total + term
        tot[q, pg] = total
        for o in FAR:
            send(tot.at[q, pg], tot.at[q, pg], t_recv.at[q, o - 1], on_g(o))

    def iterate(q):
        for o in FAR:
            wait(tot.at[q, mod4(pg + 4 - o)], t_recv.at[q, o - 1])
        scale = 0.2 * math.sqrt(max(D, HEAD))
        high, mid, low = split(newton_schulz((tot[q, 0] + tot[q, 1]) + (tot[q, 2] + tot[q, 3]), scale))
        place = pl.ds(pl.multiple_of(mycol + pr * PAIR + q * HEAD, HEAD), HEAD)
        for o in ORDER:
            first = pl.multiple_of(mod4(pr + o) * ROWS, ROWS)
            value = buf[q, pl.ds(first, ROWS), :]
            total = jnp.dot(value, low, preferred_element_type=F32) + jnp.dot(value, mid, preferred_element_type=F32)
            upd[q, pl.ds(first, ROWS), :] = (total + jnp.dot(value, high, preferred_element_type=F32)).astype(BF16)
            same = upd.at[q, pl.ds(pl.multiple_of(first + myrow, OWN), OWN)]
            cross = upd.at[q, pl.ds(pl.multiple_of(first + sibrow, OWN), OWN)]
            if o:
                send(same, upd_o.at[:, place], o_recv.at[q, 0, o], on_r(o))
                send(cross, upd_o.at[:, place], o_recv.at[q, 1, o], chip(y + o * e, x + o * c, e))
            else:
                start(pltpu.make_async_copy(same, upd_o.at[:, place], o_recv.at[q, 0, 0]))
                send(cross, upd_o.at[:, place], o_recv.at[q, 1, 0], sib)

    gram_of(0)
    chain(*PLAN[9])
    gram_of(1)
    iterate(0)
    chain(*PLAN[10])
    iterate(1)
    chain(*PLAN[12])
    for q in range(2):
        for o in range(4):
            at = pl.multiple_of(mycol + mod4(pr + 4 - o) * PAIR + q * HEAD, HEAD)
            wait(upd_o.at[:, pl.ds(at, HEAD)], o_recv.at[q, 0, o])
            at = pl.multiple_of(sibcol + mod4(pg + 4 - o) * PAIR + q * HEAD, HEAD)
            wait(upd_o.at[:, pl.ds(at, HEAD)], o_recv.at[q, 1, o])
    for cp in sends:
        cp.wait_send()

    @pl.when(z > 0)
    def _():
        @pl.loop(0, NCH)
        def _(k):
            remote(gout.at[k], gin.at[k], ch_send.at[k], ch_recv.at[k], (z - 1, d)).wait_send()


def store(upd, grads, upd_o, ig_o, sem):
    copies = [pltpu.make_async_copy(grads.at[k], ig_o.at[:, k * CH:(k + 1) * CH], sem.at[k]) for k in range(NCH)]
    copies.append(pltpu.make_async_copy(upd, upd_o, sem.at[NCH]))
    for cp in copies:
        cp.start()
    for cp in copies:
        cp.wait()


def shards(acts, cotangent, kv_grads, w_kv, momentum):
    dma = pltpu.SemaphoreType.DMA
    vmem = pltpu.VMEM
    anyspec = pl.BlockSpec(memory_space=pl.ANY)
    update, grads = pl.pallas_call(
        kernel,
        out_shape=(vmem((OWN, COLS), BF16), vmem((NCH, TOK, CH), BF16)),
        in_specs=[anyspec] * 5,
        out_specs=(pl.BlockSpec(memory_space=vmem),) * 2,
        scratch_shapes=[
            vmem((TOK, D), BF16), vmem((D, TOK), BF16), vmem((4 * ROWS, 8 * TOK), BF16),
            vmem((TOK, COLS), BF16), vmem((4, 8 * TOK, PAIR), BF16), vmem((NCH, CH, COLS), BF16),
            vmem((3, 2, 4 * ROWS, HEAD), BF16), vmem((2, 2, 2 * ROWS, HEAD), BF16), vmem((4, 4 * ROWS, PAIR), F32),
            vmem((2, 2, 4 * ROWS, HEAD), BF16), vmem((ROWS, HALF), BF16), vmem((2, 4 * ROWS, HEAD), BF16),
            vmem((2, 4, HEAD, HEAD), F32), vmem((2, 4 * ROWS, HEAD), BF16),
            vmem((NCH, TOK, CH), BF16), vmem((NCH, TOK, CH), F32),
            dma((3,)), dma((NCH,)), dma((96,)), dma((4, 4, 2)), dma((4, 2, 2)), dma((4, 4, 2)),
            dma((2, 2)), dma((2, 2)), dma((1,)), dma((NCH,)), dma((NCH,)),
            dma((2, 3)), dma((2, 2, 4)),
        ],
        name="muon_back",
        compiler_params=pltpu.CompilerParams(
            collective_id=0, has_side_effects=True, vmem_limit_bytes=56 * 1024 * 1024
        ),
    )(acts[0], cotangent, kv_grads[0], w_kv[0], momentum[0])
    update, grads = pl.pallas_call(
        store,
        out_shape=(jax.ShapeDtypeStruct((OWN, COLS), BF16), jax.ShapeDtypeStruct((TOK, D), BF16)),
        in_specs=[pl.BlockSpec(memory_space=vmem)] * 2,
        out_specs=(anyspec, anyspec),
        scratch_shapes=[dma((NCH + 1,))],
        name="store",
    )(pltpu.with_memory_space_constraint(update, vmem), pltpu.with_memory_space_constraint(grads, vmem))
    return update[None], grads[None]


def solution(mesh):
    in_specs = (
        P("pipe", "dp", None),
        P("dp", None),
        P("pipe", "dp", None),
        P("pipe", None, None),
        P("pipe", "dp", None),
    )
    out_specs = (P("pipe", "dp", None), P("pipe", "dp", None))
    return jax.shard_map(shards, mesh=mesh, in_specs=in_specs, out_specs=out_specs, check_vma=False)
```

```python
import functools
import math

import jax
import jax.numpy as jnp
from jax import lax
from jax.experimental import pallas as pl
from jax.experimental.pallas import tpu as pltpu
from jax.sharding import PartitionSpec as P

MESH = pl.DeviceIdType.MESH
F32 = jnp.float32
BF16 = jnp.bfloat16
HEAD = 128
ITERS = 5
TOK = 128
D = 5120
COLS = 2048
HALF = 1024
PAIR = 256
ROWS = 320
OWN = 160
CH = 256
NCH = D // CH
FAR = (2, 1, 3)
ORDER = (2, 1, 3, 0)
PLAN = (
    ((0, 0, 0, 2), (0, 0, 0, 2)),
    ((5, 5, 4, 8), (0, 0, 1, 8)),
    ((13, 13, 12, 20), (0, 2, 6, 20)),
    ((13, 13, 12, 20), (0, 2, 6, 20)),
    ((17, 17, 16, 20), (0, 4, 8, 20)),
    ((20, 20, 20, 20), (2, 6, 10, 20)),
    ((20, 20, 20, 20), (4, 8, 13, 20)),
    ((20, 20, 20, 20), (5, 10, 15, 20)),
    ((20, 20, 20, 20), (8, 13, 18, 20)),
    ((20, 20, 20, 20), (10, 15, 20, 20)),
    ((20, 20, 20, 20), (13, 18, 20, 20)),
    ((20, 20, 20, 20), (13, 19, 20, 20)),
    ((20, 20, 20, 20), (20, 20, 20, 20)),
    ((20, 20, 20, 20), (5, 10, 15, 20)),
    ((20, 20, 20, 20), (6, 11, 16, 20)),
    ((20, 20, 20, 20), (7, 12, 17, 20)),
    ((20, 20, 20, 20), (8, 13, 17, 20)),
)

momentum_rate = 0.95
quintic_a = 3.4445
quintic_b = -4.775
quintic_c = 2.0315
epsilon = 1e-07


def mod4(v):
    return lax.rem(v, 4)


def split(a):
    high = a.astype(BF16)
    rest = a - high.astype(F32)
    mid = rest.astype(BF16)
    return high, mid, (rest - mid.astype(F32)).astype(BF16)


def mm(sa, sb):
    a1, a2, a3 = sa
    b1, b2, b3 = sb
    right = jnp.concatenate([jnp.concatenate([b2, b3], 1), jnp.concatenate([b1, b2], 1)], 0)
    small = jnp.dot(jnp.concatenate([a1, a2], 1), right, preferred_element_type=F32)
    big = jnp.dot(jnp.concatenate([a1, a3], 1), jnp.concatenate([b1, b1], 0), preferred_element_type=F32)
    return big + (small[:, :HEAD] + small[:, HEAD:])


def newton_schulz(gram, scale):
    rows = lax.broadcasted_iota(jnp.int32, (HEAD, HEAD), 0)
    cols = lax.broadcasted_iota(jnp.int32, (HEAD, HEAD), 1)
    eye = (rows == cols).astype(F32)
    trace = jnp.sum(jnp.sum(gram * eye, axis=1, keepdims=True), axis=0, keepdims=True)
    inv = 1.0 / (jnp.sqrt(trace) + epsilon)
    a = (gram * inv) * inv
    q = None
    for step in range(ITERS):
        sa = split(a)
        m = quintic_a * eye + quintic_b * a + quintic_c * mm(sa, sa)
        sm = split(m)
        q = m if q is None else mm(split(q), sm)
        if step < ITERS - 1:
            a = mm(split(mm(sm, sa)), sm)
    return q * (inv * scale)


def kernel(
    acts_h, cot_h, kv_h, w_h, mom_h, upd_o, gout,
    acts_v, acts_t, acts_g, kv_v, kv_g, w_v, part, trans, acc, rbuf, mom_v, buf,
    tot, upd, gin, own_v,
    ld_sem, w_sem, send_sem, kv_recv, kvf_recv, ac_recv, tr_recv, rs_recv,
    mom_recv, ch_send, ch_recv, t_recv, o_recv,
):
    z = lax.axis_index("pipe")
    d = lax.axis_index("dp")
    y, x, c = lax.div(d, 8), mod4(lax.div(d, 2)), lax.rem(d, 2)
    e = 1 - c
    pg = x * e + y * c
    pr = y * e + x * c

    def chip(yy, xx, cc):
        return (z, (mod4(yy) * 4 + mod4(xx)) * 2 + cc)

    def on_g(o):
        return chip(y + o * c, x + o * e, c)

    def on_r(o):
        return chip(y + o * e, x + o * c, c)

    sib = chip(y, x, e)
    bar = pltpu.get_barrier_semaphore()

    def greet(dev):
        pl.semaphore_signal(bar, inc=1, device_id=dev, device_id_type=MESH)

    for o in FAR:
        greet(on_g(o))
        greet(chip(y + o * c, x + o * e, e))
        greet(on_r(o))
    greet(sib)

    @pl.when(z < 3)
    def _():
        greet((z + 1, d))

    def start(cp):
        cp.start()
        return cp

    def remote(src, dst, ssem, rsem, dev):
        return pltpu.make_async_remote_copy(src, dst, ssem, rsem, device_id=dev, device_id_type=MESH)

    sends = []

    def send(src, dst, rsem, dev):
        sends.append(start(remote(src, dst, send_sem.at[len(sends)], rsem, dev)))

    def wait(ref, sem):
        pltpu.make_async_copy(ref, ref, sem).wait()

    def cols(k):
        return pl.ds(pl.multiple_of(k * CH, CH), CH)

    ld_kv = start(pltpu.make_async_copy(kv_h, kv_v, ld_sem.at[0]))
    ld_acts = start(pltpu.make_async_copy(acts_h, acts_v, ld_sem.at[1]))
    myrow = pl.multiple_of(c * OWN, OWN)
    sibrow = pl.multiple_of(e * OWN, OWN)
    mycol = pl.multiple_of(c * HALF, HALF)
    sibcol = pl.multiple_of(e * HALF, HALF)
    ld_mom = start(pltpu.make_async_copy(mom_h.at[:, pl.ds(mycol, HALF)], mom_v.at[pl.ds(myrow, OWN)], ld_sem.at[2]))

    @pl.loop(0, NCH)
    def _(k):
        @pl.when(z == 3)
        def _():
            pltpu.make_async_copy(cot_h.at[:, cols(k)], gin.at[k], ch_recv.at[k]).start()

        pltpu.make_async_copy(w_h.at[pl.ds(pl.multiple_of(k * CH, CH), CH)], w_v.at[k], w_sem.at[k]).start()

    pl.semaphore_wait(bar, jnp.where(z > 0, 11, 10))

    def toks(slot, first=0, count=TOK):
        return pl.ds(pl.multiple_of(slot * TOK + first, count), count)

    slots = (x * 2 + c, y * 2 + c)
    slot_own = pg * 2 + c
    slot_sib = pr * 2 + c

    def near(off, cc):
        return mod4(pg + 4 - off) * 2 + cc

    def send_kv(o):
        at = (mod4(y + o) * PAIR, mod4(x + o) * PAIR + HALF)
        for off in (1, 3):
            for t in (0, 1):
                dev = chip(y, x + off, 0) if t == 0 else chip(y + off, x, 1)
                send(kv_v.at[:, pl.ds(pl.multiple_of(at[t], PAIR), PAIR)],
                     kv_g.at[o, toks(slots[t])], kv_recv.at[o, off, c], dev)
        own_at = pl.multiple_of(mod4(pr + o) * PAIR + mycol, PAIR)
        sib_at = pl.multiple_of(mod4(pg + o) * PAIR + sibcol, PAIR)
        start(pltpu.make_async_copy(kv_v.at[:, pl.ds(own_at, PAIR)], kv_g.at[o, toks(slot_own)], kv_recv.at[o, 0, c]))
        send(kv_v.at[:, pl.ds(sib_at, PAIR)], kv_g.at[o, toks(slot_sib)], kv_recv.at[o, 0, c], sib)

    def pass_kv(o):
        for off in (1, 3, 0):
            for cc in (0, 1):
                wait(kv_g.at[o, toks(near(off, cc))], kv_recv.at[o, off, cc])
                if off:
                    piece = kv_g.at[o, toks(near(off, cc), 0 if off == 1 else 64, 64)]
                    send(piece, piece, kvf_recv.at[o, off // 2, cc], on_g(off))

    def wait_far(o):
        for half in range(2):
            for cc in (0, 1):
                wait(kv_g.at[o, toks(near(2, cc), half * 64, 64)], kvf_recv.at[o, half, cc])

    ld_kv.wait()
    for o in FAR:
        send_kv(o)

    def product(k):
        wait(w_v.at[k], w_sem.at[k])
        own_v[k] = lax.dot_general(kv_v[...], w_v[k], (((1,), (1,)), ((), ())), preferred_element_type=F32)

    def relay(k):
        wait(gin.at[k], ch_recv.at[k])
        gout[k] = (gin[k].astype(F32) + own_v[k]).astype(BF16)

        @pl.when(z > 0)
        def _():
            remote(gout.at[k], gin.at[k], ch_send.at[k], ch_recv.at[k], (z - 1, d)).start()


    done = [0, 0]

    def chain(ahead, upto):
        ready, sent = (jnp.where(z == 0, a[0], jnp.where(z == 1, a[1], jnp.where(z == 2, a[2], a[3]))) for a in (ahead, upto))

        @pl.loop(0, jnp.maximum(ready - done[0], sent - done[1]))
        def _(n):
            @pl.when(done[0] + n < ready)
            def _():
                product(done[0] + n)

            @pl.when(done[1] + n < sent)
            def _():
                relay(done[1] + n)

        done[:] = [ready, sent]

    chain(*PLAN[0])

    send(mom_h.at[:, pl.ds(sibcol, HALF)], mom_v.at[pl.ds(myrow, OWN)], mom_recv.at[0], sib)
    ld_acts.wait()

    @pl.loop(0, D // 512)
    def _(k):
        at = pl.multiple_of(k * 512, 512)
        acts_t[pl.ds(at, 512), :] = acts_v[:, pl.ds(at, 512)].T

    def send_acts(b):
        rows = pl.ds(b * ROWS, ROWS)

        def source(block):
            return acts_t.at[pl.ds(pl.multiple_of(block * ROWS, ROWS), ROWS)]

        for off in FAR:
            for t in (0, 1):
                block, dev = (b * 4 + mod4(x + off), chip(y, x + off, 0)) if t == 0 else (mod4(y + off) * 4 + b, chip(y + off, x, 1))
                send(source(block), acts_g.at[rows, toks(slots[t])], ac_recv.at[b, off, c], dev)
        start(pltpu.make_async_copy(
            source((b * 4 + x) * e + (y * 4 + b) * c), acts_g.at[rows, toks(slot_own)], ac_recv.at[b, 0, c]))
        send(source((b * 4 + x) * c + (y * 4 + b) * e), acts_g.at[rows, toks(slot_sib)], ac_recv.at[b, 0, c], sib)

    def half_rows(half):
        return pl.ds(half * 2 * ROWS, 2 * ROWS)

    def block(o, b):
        at = pl.ds(pl.multiple_of(mod4(pr + o) * PAIR, PAIR), PAIR)
        rows = pl.ds(b * ROWS, ROWS)
        term = jnp.dot(acts_g[rows, :], kv_g[o], preferred_element_type=F32)
        term = term + (mom_v[:, at].astype(F32) * momentum_rate) * jnp.where(pr == b, 4096.0, 0.0)
        if o == 2:
            part[1, 0, rows, :] = term[:, :HEAD].astype(BF16)
            part[1, 1, rows, :] = term[:, HEAD:].astype(BF16)
        else:
            acc[o, rows, :] = term

    def transit(q, half):
        send(part.at[1, q, half_rows(half)], trans.at[q, half], tr_recv.at[q, half], on_r(1 + 2 * half))

    def near_sum(q, way, half):
        o = 1 + 2 * way
        rows = half_rows(half)
        value = acc[o, rows, q * HEAD:(q + 1) * HEAD]
        if half == way:
            value = value + trans[q, half].astype(F32)
        part[o - 1, q, rows, :] = value.astype(BF16)
        send(part.at[o - 1, q, rows], rbuf.at[q, way, rows], rs_recv.at[q, way, half], on_r(o))

    send_acts(0)
    chain(*PLAN[1])
    for o in FAR:
        pass_kv(o)
    for b in (1, 2, 3):
        send_acts(b)
    send_kv(0)
    chain(*PLAN[2])
    for o in FAR:
        wait_far(o)
    ld_mom.wait()
    wait(mom_v.at[pl.ds(sibrow, OWN)], mom_recv.at[0])
    for b in range(4):
        chain(*PLAN[3 + b])
        for off in range(4):
            for cc in (0, 1):
                wait(acts_g.at[pl.ds(b * ROWS, ROWS), toks(near(off, cc))], ac_recv.at[b, off, cc])
        block(2, b)
        block(1, b)
        block(3, b)
        if b == 1:
            for q in range(2):
                transit(q, 0)
            near_sum(0, 1, 0)
        if b == 3:
            for q in range(2):
                transit(q, 1)
            near_sum(1, 1, 0)
            near_sum(0, 0, 1)
            near_sum(1, 0, 1)
    pass_kv(0)
    chain(*PLAN[7])
    for q in range(2):
        for half in range(2):
            wait(trans.at[q, half], tr_recv.at[q, half])
            near_sum(q, half, half)
            chain(*PLAN[13 + 2 * q + half])
    wait_far(0)
    for b in range(4):
        block(0, b)
    chain(*PLAN[8])

    def gram_of(q):
        head = slice(q * HEAD, (q + 1) * HEAD)
        for way in range(2):
            for half in range(2):
                wait(rbuf.at[q, way, half_rows(half)], rs_recv.at[q, way, half])
        total = None
        for b in range(4):
            rows = pl.ds(b * ROWS, ROWS)
            grad = acc[0, rows, head] + rbuf[q, 0, rows, :].astype(F32) + rbuf[q, 1, rows, :].astype(F32)
            value = (grad * (1.0 / 4096)).astype(BF16)
            buf[q, rows, :] = value
            term = lax.dot_general(value, value, (((0,), (0,)), ((), ())), preferred_element_type=F32)
            total = term if total is None else total + term
        tot[q, pg] = total
        for o in FAR:
            send(tot.at[q, pg], tot.at[q, pg], t_recv.at[q, o - 1], on_g(o))

    def iterate(q):
        for o in FAR:
            wait(tot.at[q, mod4(pg + 4 - o)], t_recv.at[q, o - 1])
        scale = 0.2 * math.sqrt(max(D, HEAD))
        high, mid, low = split(newton_schulz((tot[q, 0] + tot[q, 1]) + (tot[q, 2] + tot[q, 3]), scale))
        place = pl.ds(pl.multiple_of(mycol + pr * PAIR + q * HEAD, HEAD), HEAD)
        for o in ORDER:
            first = pl.multiple_of(mod4(pr + o) * ROWS, ROWS)
            value = buf[q, pl.ds(first, ROWS), :]
            total = jnp.dot(value, low, preferred_element_type=F32) + jnp.dot(value, mid, preferred_element_type=F32)
            upd[q, pl.ds(first, ROWS), :] = (total + jnp.dot(value, high, preferred_element_type=F32)).astype(BF16)
            same = upd.at[q, pl.ds(pl.multiple_of(first + myrow, OWN), OWN)]
            cross = upd.at[q, pl.ds(pl.multiple_of(first + sibrow, OWN), OWN)]
            if o:
                send(same, upd_o.at[:, place], o_recv.at[q, 0, o], on_r(o))
                send(cross, upd_o.at[:, place], o_recv.at[q, 1, o], chip(y + o * e, x + o * c, e))
            else:
                start(pltpu.make_async_copy(same, upd_o.at[:, place], o_recv.at[q, 0, 0]))
                send(cross, upd_o.at[:, place], o_recv.at[q, 1, 0], sib)

    gram_of(0)
    chain(*PLAN[9])
    gram_of(1)
    iterate(0)
    chain(*PLAN[10])
    iterate(1)
    chain(*PLAN[12])
    for q in range(2):
        for o in range(4):
            at = pl.multiple_of(mycol + mod4(pr + 4 - o) * PAIR + q * HEAD, HEAD)
            wait(upd_o.at[:, pl.ds(at, HEAD)], o_recv.at[q, 0, o])
            at = pl.multiple_of(sibcol + mod4(pg + 4 - o) * PAIR + q * HEAD, HEAD)
            wait(upd_o.at[:, pl.ds(at, HEAD)], o_recv.at[q, 1, o])
    for cp in sends:
        cp.wait_send()

    @pl.when(z > 0)
    def _():
        @pl.loop(0, NCH)
        def _(k):
            remote(gout.at[k], gin.at[k], ch_send.at[k], ch_recv.at[k], (z - 1, d)).wait_send()


def store(upd, grads, upd_o, ig_o, sem):
    copies = [pltpu.make_async_copy(grads.at[k], ig_o.at[:, k * CH:(k + 1) * CH], sem.at[k]) for k in range(NCH)]
    copies.append(pltpu.make_async_copy(upd, upd_o, sem.at[NCH]))
    for cp in copies:
        cp.start()
    for cp in copies:
        cp.wait()


def shards(acts, cotangent, kv_grads, w_kv, momentum):
    dma = pltpu.SemaphoreType.DMA
    vmem = pltpu.VMEM
    anyspec = pl.BlockSpec(memory_space=pl.ANY)
    update, grads = pl.pallas_call(
        kernel,
        out_shape=(vmem((OWN, COLS), BF16), vmem((NCH, TOK, CH), BF16)),
        in_specs=[anyspec] * 5,
        out_specs=(pl.BlockSpec(memory_space=vmem),) * 2,
        scratch_shapes=[
            vmem((TOK, D), BF16), vmem((D, TOK), BF16), vmem((4 * ROWS, 8 * TOK), BF16),
            vmem((TOK, COLS), BF16), vmem((4, 8 * TOK, PAIR), BF16), vmem((NCH, CH, COLS), BF16),
            vmem((3, 2, 4 * ROWS, HEAD), BF16), vmem((2, 2, 2 * ROWS, HEAD), BF16), vmem((4, 4 * ROWS, PAIR), F32),
            vmem((2, 2, 4 * ROWS, HEAD), BF16), vmem((ROWS, HALF), BF16), vmem((2, 4 * ROWS, HEAD), BF16),
            vmem((2, 4, HEAD, HEAD), F32), vmem((2, 4 * ROWS, HEAD), BF16),
            vmem((NCH, TOK, CH), BF16), vmem((NCH, TOK, CH), F32),
            dma((3,)), dma((NCH,)), dma((104,)), dma((4, 4, 2)), dma((4, 2, 2)), dma((4, 4, 2)),
            dma((2, 2)), dma((2, 2, 2)), dma((1,)), dma((NCH,)), dma((NCH,)),
            dma((2, 3)), dma((2, 2, 4)),
        ],
        name="muon_back",
        compiler_params=pltpu.CompilerParams(
            collective_id=0, has_side_effects=True, vmem_limit_bytes=56 * 1024 * 1024
        ),
    )(acts[0], cotangent, kv_grads[0], w_kv[0], momentum[0])
    update, grads = pl.pallas_call(
        store,
        out_shape=(jax.ShapeDtypeStruct((OWN, COLS), BF16), jax.ShapeDtypeStruct((TOK, D), BF16)),
        in_specs=[pl.BlockSpec(memory_space=vmem)] * 2,
        out_specs=(anyspec, anyspec),
        scratch_shapes=[dma((NCH + 1,))],
        name="store",
    )(pltpu.with_memory_space_constraint(update, vmem), pltpu.with_memory_space_constraint(grads, vmem))
    return update[None], grads[None]


def solution(mesh):
    in_specs = (
        P("pipe", "dp", None),
        P("dp", None),
        P("pipe", "dp", None),
        P("pipe", None, None),
        P("pipe", "dp", None),
    )
    out_specs = (P("pipe", "dp", None), P("pipe", "dp", None))
    return jax.shard_map(shards, mesh=mesh, in_specs=in_specs, out_specs=out_specs, check_vma=False)
```

```python
import functools
import math

import jax
import jax.numpy as jnp
from jax import lax
from jax.experimental import pallas as pl
from jax.experimental.pallas import tpu as pltpu
from jax.sharding import PartitionSpec as P

MESH = pl.DeviceIdType.MESH
F32 = jnp.float32
BF16 = jnp.bfloat16
HEAD = 128
ITERS = 5
TOK = 128
D = 5120
COLS = 2048
HALF = 1024
PAIR = 256
ROWS = 320
OWN = 160
CH = 256
NCH = D // CH
FAR = (2, 1, 3)
ORDER = (2, 1, 3, 0)
PLAN = (
    ((0, 0, 0, 2), (0, 0, 0, 2)),
    ((5, 5, 4, 8), (0, 0, 1, 8)),
    ((13, 13, 12, 20), (0, 3, 7, 20)),
    ((13, 13, 12, 20), (0, 3, 7, 20)),
    ((17, 17, 16, 20), (0, 5, 9, 20)),
    ((20, 20, 20, 20), (2, 7, 11, 20)),
    ((20, 20, 20, 20), (4, 9, 13, 20)),
    ((20, 20, 20, 20), (5, 11, 15, 20)),
    ((20, 20, 20, 20), (8, 14, 20, 20)),
    ((20, 20, 20, 20), (11, 17, 20, 20)),
    ((20, 20, 20, 20), (13, 20, 20, 20)),
    ((20, 20, 20, 20), (13, 20, 20, 20)),
    ((20, 20, 20, 20), (20, 20, 20, 20)),
    ((20, 20, 20, 20), (5, 11, 15, 20)),
    ((20, 20, 20, 20), (6, 12, 16, 20)),
    ((20, 20, 20, 20), (7, 12, 17, 20)),
    ((20, 20, 20, 20), (8, 13, 18, 20)),
)

momentum_rate = 0.95
quintic_a = 3.4445
quintic_b = -4.775
quintic_c = 2.0315
epsilon = 1e-07


def mod4(v):
    return lax.rem(v, 4)


def split(a):
    high = a.astype(BF16)
    rest = a - high.astype(F32)
    mid = rest.astype(BF16)
    return high, mid, (rest - mid.astype(F32)).astype(BF16)


def mm(sa, sb):
    a1, a2, a3 = sa
    b1, b2, b3 = sb
    right = jnp.concatenate([jnp.concatenate([b2, b3], 1), jnp.concatenate([b1, b2], 1)], 0)
    small = jnp.dot(jnp.concatenate([a1, a2], 1), right, preferred_element_type=F32)
    big = jnp.dot(jnp.concatenate([a1, a3], 1), jnp.concatenate([b1, b1], 0), preferred_element_type=F32)
    return big + (small[:, :HEAD] + small[:, HEAD:])


def newton_schulz(gram, scale):
    rows = lax.broadcasted_iota(jnp.int32, (HEAD, HEAD), 0)
    cols = lax.broadcasted_iota(jnp.int32, (HEAD, HEAD), 1)
    eye = (rows == cols).astype(F32)
    trace = jnp.sum(jnp.sum(gram * eye, axis=1, keepdims=True), axis=0, keepdims=True)
    inv = 1.0 / (jnp.sqrt(trace) + epsilon)
    a = (gram * inv) * inv
    q = None
    for step in range(ITERS):
        sa = split(a)
        m = quintic_a * eye + quintic_b * a + quintic_c * mm(sa, sa)
        sm = split(m)
        q = m if q is None else mm(split(q), sm)
        if step < ITERS - 1:
            a = mm(split(mm(sm, sa)), sm)
    return q * (inv * scale)


def kernel(
    acts_h, cot_h, kv_h, w_h, mom_h, upd_o, gout,
    acts_v, acts_t, acts_g, kv_v, kv_g, w_v, part, trans, acc, rbuf, mom_v, buf,
    tot, upd, gin, own_v,
    ld_sem, w_sem, send_sem, kv_recv, kvf_recv, ac_recv, tr_recv, rs_recv,
    mom_recv, ch_send, ch_recv, t_recv, o_recv,
):
    z = lax.axis_index("pipe")
    d = lax.axis_index("dp")
    y, x, c = lax.div(d, 8), mod4(lax.div(d, 2)), lax.rem(d, 2)
    e = 1 - c
    pg = x * e + y * c
    pr = y * e + x * c

    def chip(yy, xx, cc):
        return (z, (mod4(yy) * 4 + mod4(xx)) * 2 + cc)

    def on_g(o):
        return chip(y + o * c, x + o * e, c)

    def on_r(o):
        return chip(y + o * e, x + o * c, c)

    sib = chip(y, x, e)
    bar = pltpu.get_barrier_semaphore()

    def greet(dev):
        pl.semaphore_signal(bar, inc=1, device_id=dev, device_id_type=MESH)

    for o in FAR:
        greet(on_g(o))
        greet(chip(y + o * c, x + o * e, e))
        greet(on_r(o))
    greet(sib)

    @pl.when(z < 3)
    def _():
        greet((z + 1, d))

    def start(cp):
        cp.start()
        return cp

    def remote(src, dst, ssem, rsem, dev):
        return pltpu.make_async_remote_copy(src, dst, ssem, rsem, device_id=dev, device_id_type=MESH)

    sends = []

    def send(src, dst, rsem, dev):
        sends.append(start(remote(src, dst, send_sem.at[len(sends)], rsem, dev)))

    def wait(ref, sem):
        pltpu.make_async_copy(ref, ref, sem).wait()

    def cols(k):
        return pl.ds(pl.multiple_of(k * CH, CH), CH)

    ld_kv = start(pltpu.make_async_copy(kv_h, kv_v, ld_sem.at[0]))
    ld_acts = start(pltpu.make_async_copy(acts_h, acts_v, ld_sem.at[1]))
    myrow = pl.multiple_of(c * OWN, OWN)
    sibrow = pl.multiple_of(e * OWN, OWN)
    mycol = pl.multiple_of(c * HALF, HALF)
    sibcol = pl.multiple_of(e * HALF, HALF)
    ld_mom = start(pltpu.make_async_copy(mom_h.at[:, pl.ds(mycol, HALF)], mom_v.at[pl.ds(myrow, OWN)], ld_sem.at[2]))

    @pl.loop(0, NCH)
    def _(k):
        @pl.when(z == 3)
        def _():
            pltpu.make_async_copy(cot_h.at[:, cols(k)], gin.at[k], ch_recv.at[k]).start()

        pltpu.make_async_copy(w_h.at[pl.ds(pl.multiple_of(k * CH, CH), CH)], w_v.at[k], w_sem.at[k]).start()

    pl.semaphore_wait(bar, jnp.where(z > 0, 11, 10))

    def toks(slot, first=0, count=TOK):
        return pl.ds(pl.multiple_of(slot * TOK + first, count), count)

    slots = (x * 2 + c, y * 2 + c)
    slot_own = pg * 2 + c
    slot_sib = pr * 2 + c

    def near(off, cc):
        return mod4(pg + 4 - off) * 2 + cc

    def send_kv(o):
        at = (mod4(y + o) * PAIR, mod4(x + o) * PAIR + HALF)
        for off in (1, 3):
            for t in (0, 1):
                dev = chip(y, x + off, 0) if t == 0 else chip(y + off, x, 1)
                send(kv_v.at[:, pl.ds(pl.multiple_of(at[t], PAIR), PAIR)],
                     kv_g.at[o, toks(slots[t])], kv_recv.at[o, off, c], dev)
        own_at = pl.multiple_of(mod4(pr + o) * PAIR + mycol, PAIR)
        sib_at = pl.multiple_of(mod4(pg + o) * PAIR + sibcol, PAIR)
        start(pltpu.make_async_copy(kv_v.at[:, pl.ds(own_at, PAIR)], kv_g.at[o, toks(slot_own)], kv_recv.at[o, 0, c]))
        send(kv_v.at[:, pl.ds(sib_at, PAIR)], kv_g.at[o, toks(slot_sib)], kv_recv.at[o, 0, c], sib)

    def pass_kv(o):
        for off in (1, 3, 0):
            for cc in (0, 1):
                wait(kv_g.at[o, toks(near(off, cc))], kv_recv.at[o, off, cc])
                if off:
                    piece = kv_g.at[o, toks(near(off, cc), 0 if off == 1 else 64, 64)]
                    send(piece, piece, kvf_recv.at[o, off // 2, cc], on_g(off))

    def wait_far(o):
        for half in range(2):
            for cc in (0, 1):
                wait(kv_g.at[o, toks(near(2, cc), half * 64, 64)], kvf_recv.at[o, half, cc])

    ld_kv.wait()
    for o in FAR:
        send_kv(o)

    def product(k):
        wait(w_v.at[k], w_sem.at[k])
        own_v[k] = lax.dot_general(kv_v[...], w_v[k], (((1,), (1,)), ((), ())), preferred_element_type=F32)

    def relay(k):
        wait(gin.at[k], ch_recv.at[k])
        gout[k] = (gin[k].astype(F32) + own_v[k]).astype(BF16)

        @pl.when(z > 0)
        def _():
            remote(gout.at[k], gin.at[k], ch_send.at[k], ch_recv.at[k], (z - 1, d)).start()


    done = [0, 0]

    def chain(ahead, upto):
        ready, sent = (jnp.where(z == 0, a[0], jnp.where(z == 1, a[1], jnp.where(z == 2, a[2], a[3]))) for a in (ahead, upto))

        @pl.loop(0, jnp.maximum(ready - done[0], sent - done[1]))
        def _(n):
            @pl.when(done[0] + n < ready)
            def _():
                product(done[0] + n)

            @pl.when(done[1] + n < sent)
            def _():
                relay(done[1] + n)

        done[:] = [ready, sent]

    chain(*PLAN[0])

    send(mom_h.at[:, pl.ds(sibcol, HALF)], mom_v.at[pl.ds(myrow, OWN)], mom_recv.at[0], sib)
    ld_acts.wait()

    @pl.loop(0, D // 512)
    def _(k):
        at = pl.multiple_of(k * 512, 512)
        acts_t[pl.ds(at, 512), :] = acts_v[:, pl.ds(at, 512)].T

    def send_acts(b):
        rows = pl.ds(b * ROWS, ROWS)

        def source(block):
            return acts_t.at[pl.ds(pl.multiple_of(block * ROWS, ROWS), ROWS)]

        for off in FAR:
            for t in (0, 1):
                block, dev = (b * 4 + mod4(x + off), chip(y, x + off, 0)) if t == 0 else (mod4(y + off) * 4 + b, chip(y + off, x, 1))
                send(source(block), acts_g.at[rows, toks(slots[t])], ac_recv.at[b, off, c], dev)
        start(pltpu.make_async_copy(
            source((b * 4 + x) * e + (y * 4 + b) * c), acts_g.at[rows, toks(slot_own)], ac_recv.at[b, 0, c]))
        send(source((b * 4 + x) * c + (y * 4 + b) * e), acts_g.at[rows, toks(slot_sib)], ac_recv.at[b, 0, c], sib)

    def half_rows(half):
        return pl.ds(half * 2 * ROWS, 2 * ROWS)

    def block(o, b):
        at = pl.ds(pl.multiple_of(mod4(pr + o) * PAIR, PAIR), PAIR)
        rows = pl.ds(b * ROWS, ROWS)
        term = jnp.dot(acts_g[rows, :], kv_g[o], preferred_element_type=F32)
        term = term + (mom_v[:, at].astype(F32) * momentum_rate) * jnp.where(pr == b, 4096.0, 0.0)
        if o == 2:
            part[1, 0, rows, :] = term[:, :HEAD].astype(BF16)
            part[1, 1, rows, :] = term[:, HEAD:].astype(BF16)
        else:
            acc[o, rows, :] = term

    def transit(q, half):
        send(part.at[1, q, half_rows(half)], trans.at[q, half], tr_recv.at[q, half], on_r(1 + 2 * half))

    def near_sum(q, way, half):
        o = 1 + 2 * way
        rows = half_rows(half)
        value = acc[o, rows, q * HEAD:(q + 1) * HEAD]
        if half == way:
            value = value + trans[q, half].astype(F32)
        part[o - 1, q, rows, :] = value.astype(BF16)
        send(part.at[o - 1, q, rows], rbuf.at[q, way, rows], rs_recv.at[q, way, half], on_r(o))

    send_acts(0)
    chain(*PLAN[1])
    for o in FAR:
        pass_kv(o)
    for b in (1, 2, 3):
        send_acts(b)
    send_kv(0)
    chain(*PLAN[2])
    for o in FAR:
        wait_far(o)
    ld_mom.wait()
    wait(mom_v.at[pl.ds(sibrow, OWN)], mom_recv.at[0])
    for b in range(4):
        chain(*PLAN[3 + b])
        for off in range(4):
            for cc in (0, 1):
                wait(acts_g.at[pl.ds(b * ROWS, ROWS), toks(near(off, cc))], ac_recv.at[b, off, cc])
        block(2, b)
        if b % 2:
            for q in range(2):
                transit(q, b // 2)
        block(1, b)
        block(3, b)
        if b == 1:
            near_sum(0, 1, 0)
        if b == 3:
            near_sum(1, 1, 0)
            near_sum(0, 0, 1)
            near_sum(1, 0, 1)
    pass_kv(0)
    chain(*PLAN[7])
    for q in range(2):
        for half in range(2):
            wait(trans.at[q, half], tr_recv.at[q, half])
            near_sum(q, half, half)
            chain(*PLAN[13 + 2 * q + half])
    wait_far(0)
    for b in range(4):
        block(0, b)
    chain(*PLAN[8])

    def gram_of(q):
        head = slice(q * HEAD, (q + 1) * HEAD)
        for way in range(2):
            for half in range(2):
                wait(rbuf.at[q, way, half_rows(half)], rs_recv.at[q, way, half])
        total = None
        for b in range(4):
            rows = pl.ds(b * ROWS, ROWS)
            grad = acc[0, rows, head] + rbuf[q, 0, rows, :].astype(F32) + rbuf[q, 1, rows, :].astype(F32)
            value = (grad * (1.0 / 4096)).astype(BF16)
            buf[q, rows, :] = value
            term = lax.dot_general(value, value, (((0,), (0,)), ((), ())), preferred_element_type=F32)
            total = term if total is None else total + term
        tot[q, pg] = total
        for o in FAR:
            send(tot.at[q, pg], tot.at[q, pg], t_recv.at[q, o - 1], on_g(o))

    def iterate(q):
        for o in FAR:
            wait(tot.at[q, mod4(pg + 4 - o)], t_recv.at[q, o - 1])
        scale = 0.2 * math.sqrt(max(D, HEAD))
        high, mid, low = split(newton_schulz((tot[q, 0] + tot[q, 1]) + (tot[q, 2] + tot[q, 3]), scale))
        wide = jnp.concatenate([high, mid], 0)
        place = pl.ds(pl.multiple_of(mycol + pr * PAIR + q * HEAD, HEAD), HEAD)
        for o in ORDER:
            first = pl.multiple_of(mod4(pr + o) * ROWS, ROWS)
            value = buf[q, pl.ds(first, ROWS), :]
            total = jnp.dot(jnp.concatenate([value, value], 1), wide, preferred_element_type=F32)
            upd[q, pl.ds(first, ROWS), :] = (total + jnp.dot(value, low, preferred_element_type=F32)).astype(BF16)
            same = upd.at[q, pl.ds(pl.multiple_of(first + myrow, OWN), OWN)]
            cross = upd.at[q, pl.ds(pl.multiple_of(first + sibrow, OWN), OWN)]
            if o:
                send(same, upd_o.at[:, place], o_recv.at[q, 0, o], on_r(o))
                send(cross, upd_o.at[:, place], o_recv.at[q, 1, o], chip(y + o * e, x + o * c, e))
            else:
                start(pltpu.make_async_copy(same, upd_o.at[:, place], o_recv.at[q, 0, 0]))
                send(cross, upd_o.at[:, place], o_recv.at[q, 1, 0], sib)

    gram_of(0)
    chain(*PLAN[9])
    gram_of(1)
    iterate(0)
    chain(*PLAN[10])
    iterate(1)
    chain(*PLAN[12])
    for q in range(2):
        for o in range(4):
            at = pl.multiple_of(mycol + mod4(pr + 4 - o) * PAIR + q * HEAD, HEAD)
            wait(upd_o.at[:, pl.ds(at, HEAD)], o_recv.at[q, 0, o])
            at = pl.multiple_of(sibcol + mod4(pg + 4 - o) * PAIR + q * HEAD, HEAD)
            wait(upd_o.at[:, pl.ds(at, HEAD)], o_recv.at[q, 1, o])
    for cp in sends:
        cp.wait_send()

    @pl.when(z > 0)
    def _():
        @pl.loop(0, NCH)
        def _(k):
            remote(gout.at[k], gin.at[k], ch_send.at[k], ch_recv.at[k], (z - 1, d)).wait_send()


def store(upd, grads, upd_o, ig_o, sem):
    copies = [pltpu.make_async_copy(grads.at[k], ig_o.at[:, k * CH:(k + 1) * CH], sem.at[k]) for k in range(NCH)]
    copies.append(pltpu.make_async_copy(upd, upd_o, sem.at[NCH]))
    for cp in copies:
        cp.start()
    for cp in copies:
        cp.wait()


def shards(acts, cotangent, kv_grads, w_kv, momentum):
    dma = pltpu.SemaphoreType.DMA
    vmem = pltpu.VMEM
    anyspec = pl.BlockSpec(memory_space=pl.ANY)
    update, grads = pl.pallas_call(
        kernel,
        out_shape=(vmem((OWN, COLS), BF16), vmem((NCH, TOK, CH), BF16)),
        in_specs=[anyspec] * 5,
        out_specs=(pl.BlockSpec(memory_space=vmem),) * 2,
        scratch_shapes=[
            vmem((TOK, D), BF16), vmem((D, TOK), BF16), vmem((4 * ROWS, 8 * TOK), BF16),
            vmem((TOK, COLS), BF16), vmem((4, 8 * TOK, PAIR), BF16), vmem((NCH, CH, COLS), BF16),
            vmem((3, 2, 4 * ROWS, HEAD), BF16), vmem((2, 2, 2 * ROWS, HEAD), BF16), vmem((4, 4 * ROWS, PAIR), F32),
            vmem((2, 2, 4 * ROWS, HEAD), BF16), vmem((ROWS, HALF), BF16), vmem((2, 4 * ROWS, HEAD), BF16),
            vmem((2, 4, HEAD, HEAD), F32), vmem((2, 4 * ROWS, HEAD), BF16),
            vmem((NCH, TOK, CH), BF16), vmem((NCH, TOK, CH), F32),
            dma((3,)), dma((NCH,)), dma((104,)), dma((4, 4, 2)), dma((4, 2, 2)), dma((4, 4, 2)),
            dma((2, 2)), dma((2, 2, 2)), dma((1,)), dma((NCH,)), dma((NCH,)),
            dma((2, 3)), dma((2, 2, 4)),
        ],
        name="muon_back",
        compiler_params=pltpu.CompilerParams(
            collective_id=0, has_side_effects=True, vmem_limit_bytes=56 * 1024 * 1024
        ),
    )(acts[0], cotangent, kv_grads[0], w_kv[0], momentum[0])
    update, grads = pl.pallas_call(
        store,
        out_shape=(jax.ShapeDtypeStruct((OWN, COLS), BF16), jax.ShapeDtypeStruct((TOK, D), BF16)),
        in_specs=[pl.BlockSpec(memory_space=vmem)] * 2,
        out_specs=(anyspec, anyspec),
        scratch_shapes=[dma((NCH + 1,))],
        name="store",
    )(pltpu.with_memory_space_constraint(update, vmem), pltpu.with_memory_space_constraint(grads, vmem))
    return update[None], grads[None]


def solution(mesh):
    in_specs = (
        P("pipe", "dp", None),
        P("dp", None),
        P("pipe", "dp", None),
        P("pipe", None, None),
        P("pipe", "dp", None),
    )
    out_specs = (P("pipe", "dp", None), P("pipe", "dp", None))
    return jax.shard_map(shards, mesh=mesh, in_specs=in_specs, out_specs=out_specs, check_vma=False)
```

```python
import functools
import math

import jax
import jax.numpy as jnp
from jax import lax
from jax.experimental import pallas as pl
from jax.experimental.pallas import tpu as pltpu
from jax.sharding import PartitionSpec as P

MESH = pl.DeviceIdType.MESH
F32 = jnp.float32
BF16 = jnp.bfloat16
HEAD = 128
ITERS = 5
TOK = 128
D = 5120
COLS = 2048
HALF = 1024
PAIR = 256
ROWS = 320
OWN = 160
CH = 256
NCH = D // CH
FAR = (2, 1, 3)
ORDER = (2, 1, 3, 0)
PLAN = (
    ((0, 0, 0, 2), (0, 0, 0, 2)),
    ((5, 5, 4, 8), (0, 0, 1, 8)),
    ((13, 13, 12, 20), (0, 3, 7, 20)),
    ((13, 13, 12, 20), (0, 3, 7, 20)),
    ((17, 17, 16, 20), (0, 5, 9, 20)),
    ((20, 20, 20, 20), (2, 7, 11, 20)),
    ((20, 20, 20, 20), (4, 9, 13, 20)),
    ((20, 20, 20, 20), (5, 11, 15, 20)),
    ((20, 20, 20, 20), (8, 14, 20, 20)),
    ((20, 20, 20, 20), (11, 17, 20, 20)),
    ((20, 20, 20, 20), (13, 20, 20, 20)),
    ((20, 20, 20, 20), (13, 20, 20, 20)),
    ((20, 20, 20, 20), (20, 20, 20, 20)),
    ((20, 20, 20, 20), (5, 11, 15, 20)),
    ((20, 20, 20, 20), (6, 12, 16, 20)),
    ((20, 20, 20, 20), (7, 12, 17, 20)),
    ((20, 20, 20, 20), (8, 13, 18, 20)),
)

momentum_rate = 0.95
quintic_a = 3.4445
quintic_b = -4.775
quintic_c = 2.0315
epsilon = 1e-07


def mod4(v):
    return lax.rem(v, 4)


def split(a):
    high = a.astype(BF16)
    rest = a - high.astype(F32)
    mid = rest.astype(BF16)
    return high, mid, (rest - mid.astype(F32)).astype(BF16)


def mm(sa, sb):
    a1, a2, a3 = sa
    b1, b2, b3 = sb
    right = jnp.concatenate([jnp.concatenate([b2, b3], 1), jnp.concatenate([b1, b2], 1)], 0)
    small = jnp.dot(jnp.concatenate([a1, a2], 1), right, preferred_element_type=F32)
    big = jnp.dot(jnp.concatenate([a1, a3], 1), jnp.concatenate([b1, b1], 0), preferred_element_type=F32)
    return big + (small[:, :HEAD] + small[:, HEAD:])


def newton_schulz(gram, scale):
    rows = lax.broadcasted_iota(jnp.int32, (HEAD, HEAD), 0)
    cols = lax.broadcasted_iota(jnp.int32, (HEAD, HEAD), 1)
    eye = (rows == cols).astype(F32)
    trace = jnp.sum(jnp.sum(gram * eye, axis=1, keepdims=True), axis=0, keepdims=True)
    inv = 1.0 / (jnp.sqrt(trace) + epsilon)
    a = (gram * inv) * inv
    q = None
    for step in range(ITERS):
        sa = split(a)
        m = quintic_a * eye + quintic_b * a + quintic_c * mm(sa, sa)
        sm = split(m)
        q = m if q is None else mm(split(q), sm)
        if step < ITERS - 1:
            a = mm(split(mm(sm, sa)), sm)
    return q * (inv * scale)


def kernel(
    acts_h, cot_h, kv_h, w_h, mom_h, upd_o, gout,
    acts_v, acts_t, acts_g, kv_v, kv_g, w_v, part, trans, acc, rbuf, mom_v, buf,
    tot, upd, gin, own_v,
    ld_sem, w_sem, send_sem, kv_recv, kvf_recv, ac_recv, tr_recv, rs_recv,
    mom_recv, ch_send, ch_recv, t_recv, o_recv,
):
    z = lax.axis_index("pipe")
    d = lax.axis_index("dp")
    y, x, c = lax.div(d, 8), mod4(lax.div(d, 2)), lax.rem(d, 2)
    e = 1 - c
    pg = x * e + y * c
    pr = y * e + x * c

    def chip(yy, xx, cc):
        return (z, (mod4(yy) * 4 + mod4(xx)) * 2 + cc)

    def on_g(o):
        return chip(y + o * c, x + o * e, c)

    def on_r(o):
        return chip(y + o * e, x + o * c, c)

    sib = chip(y, x, e)
    bar = pltpu.get_barrier_semaphore()

    def greet(dev):
        pl.semaphore_signal(bar, inc=1, device_id=dev, device_id_type=MESH)

    for o in FAR:
        greet(on_g(o))
        greet(chip(y + o * c, x + o * e, e))
        greet(on_r(o))
    greet(sib)

    @pl.when(z < 3)
    def _():
        greet((z + 1, d))

    def start(cp):
        cp.start()
        return cp

    def remote(src, dst, ssem, rsem, dev):
        return pltpu.make_async_remote_copy(src, dst, ssem, rsem, device_id=dev, device_id_type=MESH)

    sends = []

    def send(src, dst, rsem, dev):
        sends.append(start(remote(src, dst, send_sem.at[len(sends)], rsem, dev)))

    def wait(ref, sem):
        pltpu.make_async_copy(ref, ref, sem).wait()

    def cols(k):
        return pl.ds(pl.multiple_of(k * CH, CH), CH)

    ld_kv = start(pltpu.make_async_copy(kv_h, kv_v, ld_sem.at[0]))
    ld_acts = start(pltpu.make_async_copy(acts_h, acts_v, ld_sem.at[1]))
    myrow = pl.multiple_of(c * OWN, OWN)
    sibrow = pl.multiple_of(e * OWN, OWN)
    mycol = pl.multiple_of(c * HALF, HALF)
    sibcol = pl.multiple_of(e * HALF, HALF)
    ld_mom = start(pltpu.make_async_copy(mom_h.at[:, pl.ds(mycol, HALF)], mom_v.at[pl.ds(myrow, OWN)], ld_sem.at[2]))

    @pl.loop(0, NCH)
    def _(k):
        @pl.when(z == 3)
        def _():
            pltpu.make_async_copy(cot_h.at[:, cols(k)], gin.at[k], ch_recv.at[k]).start()

        pltpu.make_async_copy(w_h.at[pl.ds(pl.multiple_of(k * CH, CH), CH)], w_v.at[k], w_sem.at[k]).start()

    pl.semaphore_wait(bar, jnp.where(z > 0, 11, 10))

    def toks(slot, first=0, count=TOK):
        return pl.ds(pl.multiple_of(slot * TOK + first, count), count)

    slots = (x * 2 + c, y * 2 + c)
    slot_own = pg * 2 + c
    slot_sib = pr * 2 + c

    def near(off, cc):
        return mod4(pg + 4 - off) * 2 + cc

    def send_kv(o):
        at = (mod4(y + o) * PAIR, mod4(x + o) * PAIR + HALF)
        for off in (1, 3):
            for t in (0, 1):
                dev = chip(y, x + off, 0) if t == 0 else chip(y + off, x, 1)
                send(kv_v.at[:, pl.ds(pl.multiple_of(at[t], PAIR), PAIR)],
                     kv_g.at[o, toks(slots[t])], kv_recv.at[o, off, c], dev)
        own_at = pl.multiple_of(mod4(pr + o) * PAIR + mycol, PAIR)
        sib_at = pl.multiple_of(mod4(pg + o) * PAIR + sibcol, PAIR)
        start(pltpu.make_async_copy(kv_v.at[:, pl.ds(own_at, PAIR)], kv_g.at[o, toks(slot_own)], kv_recv.at[o, 0, c]))
        send(kv_v.at[:, pl.ds(sib_at, PAIR)], kv_g.at[o, toks(slot_sib)], kv_recv.at[o, 0, c], sib)

    def pass_kv(o):
        for off in (1, 3, 0):
            for cc in (0, 1):
                wait(kv_g.at[o, toks(near(off, cc))], kv_recv.at[o, off, cc])
                if off:
                    piece = kv_g.at[o, toks(near(off, cc), 0 if off == 1 else 64, 64)]
                    send(piece, piece, kvf_recv.at[o, off // 2, cc], on_g(off))

    def wait_far(o):
        for half in range(2):
            for cc in (0, 1):
                wait(kv_g.at[o, toks(near(2, cc), half * 64, 64)], kvf_recv.at[o, half, cc])

    ld_kv.wait()
    for o in FAR:
        send_kv(o)

    def product(k):
        wait(w_v.at[k], w_sem.at[k])
        own_v[k] = lax.dot_general(kv_v[...], w_v[k], (((1,), (1,)), ((), ())), preferred_element_type=F32)

    def relay(k):
        wait(gin.at[k], ch_recv.at[k])
        gout[k] = (gin[k].astype(F32) + own_v[k]).astype(BF16)

        @pl.when(z > 0)
        def _():
            remote(gout.at[k], gin.at[k], ch_send.at[k], ch_recv.at[k], (z - 1, d)).start()


    done = [0, 0]

    def chain(ahead, upto):
        ready, sent = (jnp.where(z == 0, a[0], jnp.where(z == 1, a[1], jnp.where(z == 2, a[2], a[3]))) for a in (ahead, upto))

        @pl.loop(0, jnp.maximum(ready - done[0], sent - done[1]))
        def _(n):
            @pl.when(done[0] + n < ready)
            def _():
                product(done[0] + n)

            @pl.when(done[1] + n < sent)
            def _():
                relay(done[1] + n)

        done[:] = [ready, sent]

    chain(*PLAN[0])

    send(mom_h.at[:, pl.ds(sibcol, HALF)], mom_v.at[pl.ds(myrow, OWN)], mom_recv.at[0], sib)
    ld_acts.wait()

    @pl.loop(0, D // 512)
    def _(k):
        at = pl.multiple_of(k * 512, 512)
        acts_t[pl.ds(at, 512), :] = acts_v[:, pl.ds(at, 512)].T

    def send_acts(b):
        rows = pl.ds(b * ROWS, ROWS)

        def source(block):
            return acts_t.at[pl.ds(pl.multiple_of(block * ROWS, ROWS), ROWS)]

        for off in FAR:
            for t in (0, 1):
                block, dev = (b * 4 + mod4(x + off), chip(y, x + off, 0)) if t == 0 else (mod4(y + off) * 4 + b, chip(y + off, x, 1))
                send(source(block), acts_g.at[rows, toks(slots[t])], ac_recv.at[b, off, c], dev)
        start(pltpu.make_async_copy(
            source((b * 4 + x) * e + (y * 4 + b) * c), acts_g.at[rows, toks(slot_own)], ac_recv.at[b, 0, c]))
        send(source((b * 4 + x) * c + (y * 4 + b) * e), acts_g.at[rows, toks(slot_sib)], ac_recv.at[b, 0, c], sib)

    def half_rows(half):
        return pl.ds(half * 2 * ROWS, 2 * ROWS)

    def block(o, b):
        at = pl.ds(pl.multiple_of(mod4(pr + o) * PAIR, PAIR), PAIR)
        rows = pl.ds(b * ROWS, ROWS)
        term = jnp.dot(acts_g[rows, :], kv_g[o], preferred_element_type=F32)
        term = term + (mom_v[:, at].astype(F32) * momentum_rate) * jnp.where(pr == b, 4096.0, 0.0)
        if o == 2:
            part[1, 0, rows, :] = term[:, :HEAD].astype(BF16)
            part[1, 1, rows, :] = term[:, HEAD:].astype(BF16)
        else:
            acc[o, rows, :] = term

    def transit(q, half):
        send(part.at[1, q, half_rows(half)], trans.at[q, half], tr_recv.at[q, half], on_r(1 + 2 * half))

    def near_sum(q, way, half):
        o = 1 + 2 * way
        rows = half_rows(half)
        value = acc[o, rows, q * HEAD:(q + 1) * HEAD]
        if half == way:
            value = value + trans[q, half].astype(F32)
        part[o - 1, q, rows, :] = value.astype(BF16)
        send(part.at[o - 1, q, rows], rbuf.at[q, way, rows], rs_recv.at[q, way, half], on_r(o))

    send_acts(0)
    chain(*PLAN[1])
    for o in FAR:
        pass_kv(o)
    for b in (1, 2, 3):
        send_acts(b)
    send_kv(0)
    chain(*PLAN[2])
    for o in FAR:
        wait_far(o)
    ld_mom.wait()
    wait(mom_v.at[pl.ds(sibrow, OWN)], mom_recv.at[0])
    for b in range(4):
        chain(*PLAN[3 + b])
        for off in range(4):
            for cc in (0, 1):
                wait(acts_g.at[pl.ds(b * ROWS, ROWS), toks(near(off, cc))], ac_recv.at[b, off, cc])
        block(2, b)
        if b % 2:
            for q in range(2):
                transit(q, b // 2)
        block(1, b)
        block(3, b)
        if b == 1:
            near_sum(0, 1, 0)
        if b == 3:
            near_sum(1, 1, 0)
            near_sum(0, 0, 1)
            near_sum(1, 0, 1)
    pass_kv(0)
    chain(*PLAN[7])
    for q in range(2):
        for half in range(2):
            wait(trans.at[q, half], tr_recv.at[q, half])
            near_sum(q, half, half)
            chain(*PLAN[13 + 2 * q + half])
    wait_far(0)
    for b in range(4):
        block(0, b)
    chain(*PLAN[8])

    def gram_of(q):
        head = slice(q * HEAD, (q + 1) * HEAD)
        for way in range(2):
            for half in range(2):
                wait(rbuf.at[q, way, half_rows(half)], rs_recv.at[q, way, half])
        total = None
        for b in range(4):
            rows = pl.ds(b * ROWS, ROWS)
            grad = acc[0, rows, head] + rbuf[q, 0, rows, :].astype(F32) + rbuf[q, 1, rows, :].astype(F32)
            value = (grad * (1.0 / 4096)).astype(BF16)
            buf[q, rows, :] = value
            term = lax.dot_general(value, value, (((0,), (0,)), ((), ())), preferred_element_type=F32)
            total = term if total is None else total + term
        tot[q, pg] = total
        for o in FAR:
            send(tot.at[q, pg], tot.at[q, pg], t_recv.at[q, o - 1], on_g(o))

    def iterate(q):
        for o in FAR:
            wait(tot.at[q, mod4(pg + 4 - o)], t_recv.at[q, o - 1])
        scale = 0.2 * math.sqrt(max(D, HEAD))
        high, mid, low = split(newton_schulz((tot[q, 0] + tot[q, 1]) + (tot[q, 2] + tot[q, 3]), scale))
        wide = jnp.concatenate([high, mid], 0)
        place = pl.ds(pl.multiple_of(mycol + pr * PAIR + q * HEAD, HEAD), HEAD)
        for o in ORDER:
            first = pl.multiple_of(mod4(pr + o) * ROWS, ROWS)
            value = buf[q, pl.ds(first, ROWS), :]
            total = jnp.dot(jnp.concatenate([value, value], 1), wide, preferred_element_type=F32)
            upd[q, pl.ds(first, ROWS), :] = (total + jnp.dot(value, low, preferred_element_type=F32)).astype(BF16)
            same = upd.at[q, pl.ds(pl.multiple_of(first + myrow, OWN), OWN)]
            cross = upd.at[q, pl.ds(pl.multiple_of(first + sibrow, OWN), OWN)]
            if o:
                send(same, upd_o.at[:, place], o_recv.at[q, 0, o], on_r(o))
                send(cross, upd_o.at[:, place], o_recv.at[q, 1, o], chip(y + o * e, x + o * c, e))
            else:
                start(pltpu.make_async_copy(same, upd_o.at[:, place], o_recv.at[q, 0, 0]))
                send(cross, upd_o.at[:, place], o_recv.at[q, 1, 0], sib)

    gram_of(0)
    chain(*PLAN[9])
    gram_of(1)
    chain(*PLAN[10])
    iterate(0)
    iterate(1)
    chain(*PLAN[12])
    for q in range(2):
        for o in range(4):
            at = pl.multiple_of(mycol + mod4(pr + 4 - o) * PAIR + q * HEAD, HEAD)
            wait(upd_o.at[:, pl.ds(at, HEAD)], o_recv.at[q, 0, o])
            at = pl.multiple_of(sibcol + mod4(pg + 4 - o) * PAIR + q * HEAD, HEAD)
            wait(upd_o.at[:, pl.ds(at, HEAD)], o_recv.at[q, 1, o])
    for cp in sends:
        cp.wait_send()

    @pl.when(z > 0)
    def _():
        @pl.loop(0, NCH)
        def _(k):
            remote(gout.at[k], gin.at[k], ch_send.at[k], ch_recv.at[k], (z - 1, d)).wait_send()


def store(upd, grads, upd_o, ig_o, sem):
    copies = [pltpu.make_async_copy(grads.at[k], ig_o.at[:, k * CH:(k + 1) * CH], sem.at[k]) for k in range(NCH)]
    copies.append(pltpu.make_async_copy(upd, upd_o, sem.at[NCH]))
    for cp in copies:
        cp.start()
    for cp in copies:
        cp.wait()


def shards(acts, cotangent, kv_grads, w_kv, momentum):
    dma = pltpu.SemaphoreType.DMA
    vmem = pltpu.VMEM
    anyspec = pl.BlockSpec(memory_space=pl.ANY)
    update, grads = pl.pallas_call(
        kernel,
        out_shape=(vmem((OWN, COLS), BF16), vmem((NCH, TOK, CH), BF16)),
        in_specs=[anyspec] * 5,
        out_specs=(pl.BlockSpec(memory_space=vmem),) * 2,
        scratch_shapes=[
            vmem((TOK, D), BF16), vmem((D, TOK), BF16), vmem((4 * ROWS, 8 * TOK), BF16),
            vmem((TOK, COLS), BF16), vmem((4, 8 * TOK, PAIR), BF16), vmem((NCH, CH, COLS), BF16),
            vmem((3, 2, 4 * ROWS, HEAD), BF16), vmem((2, 2, 2 * ROWS, HEAD), BF16), vmem((4, 4 * ROWS, PAIR), F32),
            vmem((2, 2, 4 * ROWS, HEAD), BF16), vmem((ROWS, HALF), BF16), vmem((2, 4 * ROWS, HEAD), BF16),
            vmem((2, 4, HEAD, HEAD), F32), vmem((2, 4 * ROWS, HEAD), BF16),
            vmem((NCH, TOK, CH), BF16), vmem((NCH, TOK, CH), F32),
            dma((3,)), dma((NCH,)), dma((104,)), dma((4, 4, 2)), dma((4, 2, 2)), dma((4, 4, 2)),
            dma((2, 2)), dma((2, 2, 2)), dma((1,)), dma((NCH,)), dma((NCH,)),
            dma((2, 3)), dma((2, 2, 4)),
        ],
        name="muon_back",
        compiler_params=pltpu.CompilerParams(
            collective_id=0, has_side_effects=True, vmem_limit_bytes=56 * 1024 * 1024
        ),
    )(acts[0], cotangent, kv_grads[0], w_kv[0], momentum[0])
    update, grads = pl.pallas_call(
        store,
        out_shape=(jax.ShapeDtypeStruct((OWN, COLS), BF16), jax.ShapeDtypeStruct((TOK, D), BF16)),
        in_specs=[pl.BlockSpec(memory_space=vmem)] * 2,
        out_specs=(anyspec, anyspec),
        scratch_shapes=[dma((NCH + 1,))],
        name="store",
    )(pltpu.with_memory_space_constraint(update, vmem), pltpu.with_memory_space_constraint(grads, vmem))
    return update[None], grads[None]


def solution(mesh):
    in_specs = (
        P("pipe", "dp", None),
        P("dp", None),
        P("pipe", "dp", None),
        P("pipe", None, None),
        P("pipe", "dp", None),
    )
    out_specs = (P("pipe", "dp", None), P("pipe", "dp", None))
    return jax.shard_map(shards, mesh=mesh, in_specs=in_specs, out_specs=out_specs, check_vma=False)
```
